512 devices in a mesh: dp: 16 (over y, x_hi, core), ctx: 32 (over z, x_lo).
Axes of the slice: x: 4 (x_hi: 2, x_lo: 2; x = x_hi * 2 + x_lo), y: 4, z: 16, core: 2. Of those that a mesh axis runs over, the one named last changes fastest.
Arguments:
- queries: bfloat16 [16, 4096, 2048], P('dp', 'ctx'), may hold values from -64 to 64
- key_states: bfloat16 [16, 4096, 1024], P('dp', 'ctx'), may hold values from -6 to 6
- value_states: bfloat16 [16, 4096, 1024], P('dp', 'ctx'), may hold values from -6 to 6
- cotangent: bfloat16 [16, 4096, 5376], P('dp', 'ctx'), may hold values from -96 to 96
- core_aux: bfloat16 [16, 42, 8], replicated, may hold values from -0.5 to 0.5
- core_central: bfloat16 [8, 128, 128], replicated, may hold values from -0.5 to 0.5
Outputs:
- grad_queries: bfloat16 [16, 4096, 2048], P('dp', 'ctx')
- grad_keys: bfloat16 [16, 4096, 1024], P('dp', 'ctx')
- grad_values: bfloat16 [16, 4096, 1024], P('dp', 'ctx')
- grad_core: float32 [16, 42, 8], replicated
The draws below stay inside these ranges and needn't reach their ends.
All inputs are finite; a program needn't handle non-finite values.
Results may differ from the reference program's by a relative error of at most 0.014.
The reference program's roundings to bfloat16 on the way count: a program that leaves them out, or rounds other values in their place, can miss the bound.
Values may be sent and summed in bfloat16 or wider, within the bound.
A program may use at most 128 MiB of HBM per device.

```python
import jax
import jax.numpy as jnp
from jax import lax

D = 5376
HD = 128
HQ = 16
HK = 8
J2 = 128
J1 = 42
BOND = 8
WINDOW = 1024
TOK_DEV = 128
LENGTH = 4096
SEQS = 16


def shared_keys(key):
    shape = (SEQS, LENGTH, HK * HD)
    draws = jnp.clip(jax.random.normal(jax.random.fold_in(key, 11), shape, jnp.float32), -6.0, 6.0)
    return draws


def draw_key_states(key, part):
    return shared_keys(key).astype(jnp.bfloat16)


def draw_queries(key, part):
    shape = (SEQS, LENGTH, HQ * HD)
    draws = jnp.clip(jax.random.normal(jax.random.fold_in(key, 21), shape, jnp.float32), -6.0, 6.0)
    return draws.astype(jnp.bfloat16)


def levels(stream_key, shape, pieces, least, top_value):
    def one(dim, shards_of):
        steps = jax.random.uniform(jax.random.fold_in(jax.random.fold_in(stream_key, 6), dim), (shards_of,), jnp.float32, least / len(pieces), top_value / len(pieces))
        return jnp.repeat(jnp.exp(steps), shape[dim] // shards_of).reshape((-1,) + (1,) * (len(shape) - dim - 1))

    level = one(*pieces[0])
    for cut in pieces[1:]:
        level = level * one(*cut)
    return level


def normal_values(key, shape, scale, limit, pieces=(), kind=jnp.bfloat16):
    array = jax.random.normal(key, shape, jnp.float32) * scale
    if len(pieces) > 0:
        array = levels(key, shape, pieces, -0.22, 0.18) * array
    return jnp.clip(array, min=-limit, max=limit).astype(kind)


def setup_inputs(seed: int = 0) -> dict:
    seeds = jax.random.split(jax.random.key(seed), 7)
    return {
        "queries": draw_queries(jax.random.fold_in(seeds[6], 71), 0),
        "key_states": draw_key_states(jax.random.fold_in(seeds[6], 71), 0),
        "value_states": normal_values(seeds[2], (SEQS, LENGTH, HK * HD), 1.0, 6.0, ((0, 16), (1, 32))),
        "cotangent": normal_values(seeds[3], (SEQS, LENGTH, D), 16.0, 96.0, ((0, 16), (1, 32))),
        "core_aux": normal_values(seeds[4], (HQ, J1, BOND), (HQ * BOND) ** -0.5, 0.5),
        "core_central": normal_values(seeds[5], (BOND, HD, J2), HD ** -0.5, 0.5),
    }


SCORE_SCALE = 168.0 ** (-0.5)
MASK_FILL = -1e+30

def block_terms(query_rows, key_win, value_win, cot_rows, core_aux, core_central, first_pos):
    tok_rows = query_rows.shape[0]
    reach_blocks = WINDOW // tok_rows
    extent = key_win.shape[0]
    group_size = HQ // HK
    query_heads = query_rows.astype(jnp.float32).reshape(tok_rows, HK, group_size, HD)
    key_heads = key_win.astype(jnp.float32).reshape(extent, HK, HD)
    value_heads = value_win.astype(jnp.float32).reshape(extent, HK, HD)
    scores = jnp.einsum('tkgd,rkd->kgtr', query_heads, key_heads) * SCORE_SCALE
    query_pos = first_pos + jnp.arange(tok_rows, dtype=jnp.int32)
    key_pos = first_pos - reach_blocks * tok_rows + jnp.arange(extent, dtype=jnp.int32)
    pos_gap = query_pos[:, None] - key_pos[None, :]
    allowed = (pos_gap >= 0) & (pos_gap < WINDOW) & (key_pos[None, :] >= 0)
    scores = jnp.where(allowed, scores, MASK_FILL)
    row_max = lax.optimization_barrier(jnp.max(scores, axis=-1, keepdims=True))
    exp_terms = jnp.exp(scores - row_max)
    attn_prob = exp_terms / lax.optimization_barrier(jnp.sum(exp_terms, axis=-1, keepdims=True))
    prob_half = attn_prob.astype(jnp.bfloat16).astype(jnp.float32)
    attn = jnp.einsum('kgtr,rkd->tkgd', prob_half, value_heads).reshape(tok_rows, HQ * HD).astype(jnp.bfloat16)
    cot_split = cot_rows.astype(jnp.float32).reshape(tok_rows, J1, J2)
    hidden = jnp.einsum('tjc,bpc->tjbp', cot_split, core_central.astype(jnp.float32))
    hidden = hidden.astype(jnp.bfloat16).astype(jnp.float32)
    attn_heads = attn.astype(jnp.float32).reshape(tok_rows, HQ, HD)
    grad_part = jnp.einsum('tip,tjbp->ijb', attn_heads, hidden)
    d_attn = jnp.einsum('ijb,tjbp->tip', core_aux.astype(jnp.float32), hidden)
    d_attn = d_attn.astype(jnp.bfloat16).astype(jnp.float32).reshape(tok_rows, HK, group_size, HD)
    attn_group = attn_heads.reshape(tok_rows, HK, group_size, HD)
    d_prob = jnp.einsum('tkgd,rkd->kgtr', d_attn, value_heads)
    row_delta = jnp.einsum('tkgd,tkgd->kgt', d_attn, attn_group)
    d_score = (attn_prob * (d_prob - row_delta[..., None])).astype(jnp.bfloat16).astype(jnp.float32)
    grad_query = (jnp.einsum('kgtr,rkd->tkgd', d_score, key_heads) * SCORE_SCALE).reshape(tok_rows, HQ * HD)
    grad_key = jnp.einsum('kgtr,tkgd->rkd', d_score, query_heads).reshape(extent, HK * HD) * SCORE_SCALE
    grad_value = jnp.einsum('kgtr,tkgd->rkd', prob_half, d_attn).reshape(extent, HK * HD)
    return (grad_query.astype(jnp.bfloat16), grad_key.astype(jnp.bfloat16), grad_value.astype(jnp.bfloat16), grad_part)

def reference(queries, key_states, value_states, cotangent, core_aux, core_central):
    tok_rows = TOK_DEV
    reach_blocks = WINDOW // tok_rows
    extent = (reach_blocks + 1) * tok_rows
    kv_width = HK * HD

    def one_sequence(seq_items):
        query_seq, key_seq, value_seq, cot_seq = seq_items
        padding = jnp.zeros((reach_blocks * tok_rows, kv_width), key_seq.dtype)
        key_pad = jnp.concatenate([padding, key_seq], 0)
        value_pad = jnp.concatenate([padding, value_seq], 0)

        def block_step(state_acc, block_idx):
            key_acc, value_acc, core_acc = state_acc
            row_start = (block_idx * tok_rows).astype(jnp.int32)
            query_rows = lax.dynamic_slice_in_dim(query_seq, row_start, tok_rows, 0)
            cot_rows = lax.dynamic_slice_in_dim(cot_seq, row_start, tok_rows, 0)
            key_win = lax.dynamic_slice_in_dim(key_pad, row_start, extent, 0)
            value_win = lax.dynamic_slice_in_dim(value_pad, row_start, extent, 0)
            grad_query, grad_key, grad_value, grad_part = block_terms(query_rows, key_win, value_win, cot_rows, core_aux, core_central, row_start)
            key_acc = lax.dynamic_update_slice_in_dim(key_acc, lax.dynamic_slice_in_dim(key_acc, row_start, extent, 0) + grad_key.astype(jnp.float32), row_start, 0)
            value_acc = lax.dynamic_update_slice_in_dim(value_acc, lax.dynamic_slice_in_dim(value_acc, row_start, extent, 0) + grad_value.astype(jnp.float32), row_start, 0)
            return ((key_acc, value_acc, core_acc + grad_part), grad_query)
        initial = (jnp.zeros((LENGTH + reach_blocks * tok_rows, kv_width), jnp.float32), jnp.zeros((LENGTH + reach_blocks * tok_rows, kv_width), jnp.float32), jnp.zeros((HQ, J1, BOND), jnp.float32))
        final, grad_query = lax.scan(block_step, initial, jnp.arange(LENGTH // tok_rows, dtype=jnp.int32))
        key_acc, value_acc, core_acc = final
        return (grad_query.reshape(LENGTH, HQ * HD), key_acc[reach_blocks * tok_rows:].astype(jnp.bfloat16), value_acc[reach_blocks * tok_rows:].astype(jnp.bfloat16), core_acc)
    grad_queries, grad_keys, grad_values, core_parts = lax.map(one_sequence, (queries, key_states, value_states, cotangent))
    grad_core = lax.optimization_barrier(jnp.sum(core_parts, axis=0)) / jnp.sqrt(jnp.float32(SEQS * LENGTH * HD))
    return (grad_queries, grad_keys, grad_values, grad_core)
```

```python
import functools
import math

import jax
import jax.numpy as jnp
from jax import lax
from jax.experimental import pallas as pl
from jax.experimental.pallas import tpu as pltpu
from jax.sharding import PartitionSpec as P

HD = 128
HQ = 16
HK = 8
J1 = 42
JP = 48
BOND = 8
WINDOW = 1024
TOK = 128
BLK = 2 * TOK
OWN = HK // 2
HOPS = WINDOW // BLK
COLS = 2 * BLK
SCORE_SCALE = 168.0 ** (-0.5)
EXP_SCALE = SCORE_SCALE * math.log2(math.e)
MASK_FILL = -1e30
F32 = jnp.float32
BF16 = jnp.bfloat16
MESH = pl.DeviceIdType.MESH


def reduce_stages(mesh_shape):
    stages = []
    for axis in ("dp", "ctx"):
        bits = mesh_shape[axis].bit_length() - 1
        shift = 0
        while bits > 0:
            take = min(2, bits)
            stages.append((axis, shift, 1 << take))
            shift += take
            bits -= take
    return stages


def nt(a, b):
    return lax.dot_general(a, b, (((1,), (1,)), ((), ())), preferred_element_type=F32)


def nn(a, b):
    return lax.dot_general(a, b, (((1,), (0,)), ((), ())), preferred_element_type=F32)


def lanes(start):
    return pl.ds(pl.multiple_of(start * HD, HD), HD)


def rows(start):
    return pl.ds(pl.multiple_of(start * TOK, TOK), TOK)


def kernel(
    n_ctx, stages,
    q_ref, k_ref, v_ref, cot_ref, aux_ref, cen_ref,
    dq_ref, dk_ref, dv_ref, core_ref,
    kv, qbuf, dabuf, dasend, atx, atin, dqx, csend, crecv, finx, arbuf,
    cots, est, mat, cent, kt, vt, dat, sc, ph, ds, part,
    kx_s, kx_r, loc, qx_s, qx_r, qloc, hop_s, hop_r, da_s, da_r, at_s, at_r,
    dq_s, dq_r, ch_s, ch_r, fin_s, fin_r, ar_s, ar_r,
):
    me_dp = lax.axis_index("dp")
    me = lax.axis_index("ctx")
    zpos = me // 2
    xlo = lax.rem(me, 2)
    other = 1 - xlo
    partner = {"ctx": me + 1 - 2 * xlo}
    up = {"ctx": lax.rem(me + 2, n_ctx)}
    down = {"ctx": lax.rem(me + n_ctx - 2, n_ctx)}
    at_axis = {"dp": me_dp, "ctx": me}

    def stage_peers(stage):
        axis, shift, size = stage
        here = at_axis[axis]
        pos = lax.rem(here // (1 << shift), size)
        out = []
        for d in range(1, size):
            their = lax.rem(pos + d, size)
            out.append((d, {axis: here + (their - pos) * (1 << shift)}))
        return pos, out

    def remote(src, dst, s, r, dev):
        return pltpu.make_async_remote_copy(
            src_ref=src, dst_ref=dst, send_sem=s, recv_sem=r, device_id=dev, device_id_type=MESH
        )

    barrier = pltpu.get_barrier_semaphore()
    greet = [partner, up, down]
    for stage in stages:
        greet += [dev for _, dev in stage_peers(stage)[1]]
    for dev in greet:
        pl.semaphore_signal(barrier, inc=1, device_id=dev, device_id_type=MESH)
    pl.semaphore_wait(barrier, len(greet))

    srcs = (k_ref, v_ref)

    def kx(h, c):
        return remote(
            srcs[c].at[:, lanes(other * OWN + h)], kv.at[0, h, c, rows(xlo)],
            kx_s.at[h, c], kx_r.at[h, c], partner,
        )

    def kloc(h, c):
        return pltpu.make_async_copy(
            srcs[c].at[:, lanes(xlo * OWN + h)], kv.at[0, h, c, rows(xlo)], loc.at[h, c]
        )

    def qx(h, g):
        return remote(
            q_ref.at[:, lanes(other * 2 * OWN + 2 * h + g)], qbuf.at[h, rows(2 * g + xlo)],
            qx_s.at[h, g], qx_r.at[h, g], partner,
        )

    def qlocal(h, g):
        return pltpu.make_async_copy(
            q_ref.at[:, lanes(xlo * 2 * OWN + 2 * h + g)], qbuf.at[h, rows(2 * g + xlo)], qloc.at[h, g]
        )

    def hop(s, h):
        return remote(kv.at[s - 1, h], kv.at[s, h], hop_s.at[s - 1, h], hop_r.at[s - 1, h], up)

    def dax(h, g):
        return remote(
            dasend.at[h, g], dabuf.at[h, rows(2 * g + xlo)], da_s.at[h, g], da_r.at[h, g], partner
        )

    def attnx(h, g):
        return remote(
            atx.at[h, rows(2 * g + other)], atin.at[h, g], at_s.at[h, g], at_r.at[h, g], partner
        )

    def dqxc(h, g):
        return remote(
            dqx.at[h, rows(2 * g + other)], dq_ref.at[:, lanes(xlo * 2 * OWN + 2 * h + g)],
            dq_s.at[h, g], dq_r.at[h, g], partner,
        )

    def chain(st, h):
        return remote(csend.at[st, h], crecv.at[st, h], ch_s.at[st, h], ch_r.at[st, h], down)

    outs = (dk_ref, dv_ref)

    def finc(h, c):
        return remote(
            finx.at[h, c], outs[c].at[:, lanes(xlo * OWN + h)], fin_s.at[h, c], fin_r.at[h, c], partner
        )

    for h in range(OWN):
        for c in range(2):
            kx(h, c).start()
            kloc(h, c).start()
    for h in range(OWN):
        for c in range(2):
            qx(h, c).start()
            qlocal(h, c).start()

    for t_pad in range(1):
        @pl.loop(0, TOK)
        def _(t):
            cots[pl.ds(t * JP + JP - 8, 8), :] = jnp.zeros((8, HD), F32)

    @pl.loop(0, J1)
    def _(j):
        cots[pl.ds(j, TOK, stride=JP), :] = cot_ref[:, lanes(j)].astype(F32)

    @pl.loop(0, BOND)
    def _(b):
        cent[rows(b), :] = cen_ref[b].T

    def cot_tok(t):
        return cots[pl.ds(pl.multiple_of(t * JP, JP), JP), :].astype(BF16)

    def e_terms(t):
        e = nn(aux_ref[...], cot_tok(t)).astype(BF16)
        r16 = pl.ds(pl.multiple_of(t * HQ, HQ), HQ)
        for b in range(BOND):
            est[r16, b * HD : (b + 1) * HD] = e[b * HQ : (b + 1) * HQ]

    order = sorted(((s, h) for s in range(1, HOPS + 1) for h in range(OWN)), key=lambda a: (a[0] + a[1], -a[0]))
    per = TOK // len(order)
    for n, (s, h) in enumerate(order):
        if s == 1:
            for c in range(2):
                kx(h, c).wait_recv()
                kloc(h, c).wait()
        else:
            hop(s - 1, h).wait_recv()
        hop(s, h).start()

        @pl.loop(n * per, (n + 1) * per, unroll=4)
        def _(t):
            e_terms(t)

    @pl.loop(0, 8)
    def _(n):
        rr = pl.ds(pl.multiple_of(n * 256, 256), 256)
        mat[rr, :] = nn(est[rr, :], cent[...]).astype(BF16).astype(F32)

    for h in range(OWN):
        for g in range(2):
            i_other = other * 2 * OWN + 2 * h + g
            dasend[h, g] = mat[pl.ds(i_other, TOK, stride=HQ), :].astype(BF16)
    for h in range(OWN):
        for g in range(2):
            dax(h, g).start()
    for h in range(OWN):
        for g in range(2):
            i_own = xlo * 2 * OWN + 2 * h + g
            dabuf[h, rows(2 * g + xlo)] = mat[pl.ds(i_own, TOK, stride=HQ), :].astype(BF16)

    for h in range(OWN):
        for g in range(2):
            qx(h, g).wait_recv()
            qlocal(h, g).wait()
            dax(h, g).wait_recv()

    t_pos = lax.rem(lax.broadcasted_iota(jnp.int32, (TOK, COLS), 1), BLK)
    r_iota = lax.broadcasted_iota(jnp.int32, (TOK, COLS), 0)

    def service(n):
        for st in range(HOPS + 1):
            hh = n - st

            @pl.when(jnp.logical_and(hh >= 0, hh < OWN))
            def _():
                if st == 0:
                    total = part[hh, HOPS]
                else:
                    chain(st - 1, hh).wait_recv()
                    total = crecv[st - 1, hh].astype(F32) + part[hh, HOPS - st]
                total = total.astype(BF16)
                if st < HOPS:
                    csend[st, hh] = total
                    chain(st, hh).start()
                else:
                    part[hh, 0] = total.astype(F32)
                    for c in range(2):
                        finx[hh, c] = part[hh, 0, c, rows(other)].astype(BF16)
                        finc(hh, c).start()
                        outs[c][:, lanes(xlo * OWN + hh)] = part[hh, 0, c, rows(xlo)].astype(BF16)

    @pl.loop(0, OWN)
    def _(h):
        hop(HOPS, h).wait_recv()
        qh = qbuf[h]
        dah = dabuf[h]
        dat[...] = dah.T
        for s in range(HOPS + 1):
            for u in range(2):
                w = 2 * s + u
                kt[:, w * TOK : (w + 1) * TOK] = kv[s, h, 0, u * TOK : (u + 1) * TOK].T
                vt[:, w * TOK : (w + 1) * TOK] = kv[s, h, 1, u * TOK : (u + 1) * TOK].T

        def scores(s, u):
            return nt(kv[s, h, 0, rows(u)], qh)

        m = jnp.full((1, COLS), MASK_FILL, F32)
        for u in range(2):
            causal = t_pos >= r_iota + u * TOK
            far = jnp.where(zpos >= HOPS, scores(HOPS, u), MASK_FILL)
            x = jnp.where(causal, scores(0, u), far)
            sc[u * TOK : (u + 1) * TOK, :] = x
            m = jnp.maximum(m, jnp.max(x, axis=0, keepdims=True))

        def score_step(w, m):
            s = w // 2
            x = jnp.where(zpos >= s, scores(s, lax.rem(w, 2)), MASK_FILL)
            sc[rows(w), :] = x
            return jnp.maximum(m, jnp.max(x, axis=0, keepdims=True))

        m = lax.fori_loop(2, 2 * HOPS, score_step, m)

        def exp_step(w, l):
            e = jnp.exp2((sc[rows(w), :] - m) * EXP_SCALE)
            sc[rows(w), :] = e
            return l + jnp.sum(e, axis=0, keepdims=True)

        l = lax.fori_loop(0, 2 * HOPS, exp_step, jnp.zeros((1, COLS), F32))
        inv = 1.0 / l

        for u in range(2):
            causal = t_pos >= r_iota + u * TOK
            p = sc[u * TOK : (u + 1) * TOK, :] * inv
            sc[u * TOK : (u + 1) * TOK, :] = p
            ph[u * TOK : (u + 1) * TOK, :] = jnp.where(causal, p, 0.0).astype(BF16)
            w = 2 * HOPS + u
            ph[w * TOK : (w + 1) * TOK, :] = jnp.where(causal, 0.0, p).astype(BF16)

        @pl.loop(2, 2 * HOPS)
        def _(w):
            p = sc[rows(w), :] * inv
            sc[rows(w), :] = p
            ph[rows(w), :] = p.astype(BF16)

        att = nn(vt[...], ph[...]).astype(BF16)
        delta = jnp.sum(att.astype(F32) * dat[...].astype(F32), axis=0, keepdims=True)
        atx[h] = att.T
        for g in range(2):
            attnx(h, g).start()

        def dprob(s, u):
            return nn(kv[s, h, 1, rows(u)], dat[...])

        for u in range(2):
            causal = t_pos >= r_iota + u * TOK
            dp = jnp.where(causal, dprob(0, u), dprob(HOPS, u))
            d = sc[u * TOK : (u + 1) * TOK, :] * (dp - delta)
            ds[u * TOK : (u + 1) * TOK, :] = jnp.where(causal, d, 0.0).astype(BF16)
            w = 2 * HOPS + u
            ds[w * TOK : (w + 1) * TOK, :] = jnp.where(causal, 0.0, d).astype(BF16)

        @pl.loop(2, 2 * HOPS)
        def _(w):
            dp = dprob(w // 2, lax.rem(w, 2))
            ds[rows(w), :] = (sc[rows(w), :] * (dp - delta)).astype(BF16)

        dqt = (nn(kt[...], ds[...]) * SCORE_SCALE).astype(BF16)
        dqx[h] = dqt.T
        for g in range(2):
            dqxc(h, g).start()
        for g in range(2):
            dq_ref[:, lanes(xlo * 2 * OWN + 2 * h + g)] = dqx[h, rows(2 * g + xlo)]

        @pl.loop(0, HOPS + 1)
        def _(s):
            for u in range(2):
                rr = rows(2 * s + u)
                part[h, s, 0, u * TOK : (u + 1) * TOK] = nn(ds[rr, :], qh) * SCORE_SCALE
                part[h, s, 1, u * TOK : (u + 1) * TOK] = nn(ph[rr, :], dah)

        service(h)

    service(OWN)

    for h in range(OWN):
        for g in range(2):
            i_own = xlo * 2 * OWN + 2 * h + g
            mat[pl.ds(i_own, TOK, stride=HQ), :] = atx[h, rows(2 * g + xlo)].astype(F32)
    for h in range(OWN):
        for g in range(2):
            attnx(h, g).wait_recv()
            i_other = other * 2 * OWN + 2 * h + g
            mat[pl.ds(i_other, TOK, stride=HQ), :] = atin[h, g].astype(F32)

    @pl.loop(0, 8)
    def _(n):
        rr = pl.ds(pl.multiple_of(n * 256, 256), 256)
        a = mat[rr, :].astype(BF16)
        for b in range(BOND):
            est[rr, b * HD : (b + 1) * HD] = nn(a, cen_ref[b]).astype(BF16)

    service(OWN + 1)

    def core_step(t, acc):
        r16 = pl.ds(pl.multiple_of(t * HQ, HQ), HQ)
        f = jnp.concatenate([est[r16, b * HD : (b + 1) * HD] for b in range(BOND)], axis=0)
        return acc + nt(cot_tok(t), f)

    core_ref[...] = lax.fori_loop(0, TOK, core_step, jnp.zeros((JP, BOND * HQ), F32), unroll=4)

    for k, stage in enumerate(stages):
        pos, peers = stage_peers(stage)
        arbuf[k, pos] = core_ref[...]

        def copy(d, dev):
            return remote(arbuf.at[k, pos], arbuf.at[k, pos], ar_s.at[k, d], ar_r.at[k, d], dev)

        for d, dev in peers:
            copy(d, dev).start()
        if k < OWN - 2:
            service(OWN + 2 + k)
        for d, dev in peers:
            copy(d, dev).wait_recv()
        total = arbuf[k, 0]
        for n in range(1, stage[2]):
            total = total + arbuf[k, n]
        core_ref[...] = total
        for d, dev in peers:
            copy(d, dev).wait_send()
    for k in range(max(0, min(OWN - 2, len(stages))), OWN - 2):
        service(OWN + 2 + k)

    for h in range(OWN):
        for c in range(2):
            kx(h, c).wait_send()
            qx(h, c).wait_send()
            dax(h, c).wait_send()
            attnx(h, c).wait_send()
            dqxc(h, c).wait()
            finc(h, c).wait()
        for s in range(HOPS):
            hop(s + 1, h).wait_send()
            chain(s, h).wait_send()


def solution(mesh):
    n_ctx = mesh.shape["ctx"]
    stages = reduce_stages(mesh.shape)
    all_tokens = TOK * n_ctx * mesh.shape["dp"]

    def step(queries, key_states, value_states, cotangent, core_aux, core_central):
        aux = jnp.transpose(core_aux, (2, 0, 1)).reshape(BOND * HQ, J1)
        aux = jnp.pad(aux, ((0, 0), (0, JP - J1)))
        vm = pl.BlockSpec(memory_space=pltpu.VMEM)
        dma = pltpu.SemaphoreType.DMA
        pair = dma((OWN, 2))
        width = 2 * OWN * HD
        most = max(size for _, _, size in stages)
        dq, dk, dv, core = pl.pallas_call(
            functools.partial(kernel, n_ctx, stages),
            out_shape=(
                jax.ShapeDtypeStruct((TOK, HQ * HD), BF16),
                jax.ShapeDtypeStruct((TOK, HK * HD), BF16),
                jax.ShapeDtypeStruct((TOK, HK * HD), BF16),
                jax.ShapeDtypeStruct((JP, BOND * HQ), F32),
            ),
            in_specs=[vm] * 6,
            out_specs=(vm, vm, vm, vm),
            scratch_shapes=[
                pltpu.VMEM((HOPS + 1, OWN, 2, BLK, HD), BF16),
                pltpu.VMEM((OWN, COLS, HD), BF16),
                pltpu.VMEM((OWN, COLS, HD), BF16),
                pltpu.VMEM((OWN, 2, TOK, HD), BF16),
                pltpu.VMEM((OWN, COLS, HD), BF16),
                pltpu.VMEM((OWN, 2, TOK, HD), BF16),
                pltpu.VMEM((OWN, COLS, HD), BF16),
                pltpu.VMEM((HOPS, OWN, 2, BLK, HD), BF16),
                pltpu.VMEM((HOPS, OWN, 2, BLK, HD), BF16),
                pltpu.VMEM((OWN, 2, TOK, HD), BF16),
                pltpu.VMEM((len(stages), most, JP, BOND * HQ), F32),
                pltpu.VMEM((TOK * JP, HD), F32),
                pltpu.VMEM((TOK * HQ, BOND * HD), BF16),
                pltpu.VMEM((TOK * HQ, HD), F32),
                pltpu.VMEM((BOND * HD, HD), BF16),
                pltpu.VMEM((HD, (HOPS + 1) * BLK), BF16),
                pltpu.VMEM((HD, (HOPS + 1) * BLK), BF16),
                pltpu.VMEM((HD, COLS), BF16),
                pltpu.VMEM((HOPS * BLK, COLS), F32),
                pltpu.VMEM(((HOPS + 1) * BLK, COLS), BF16),
                pltpu.VMEM(((HOPS + 1) * BLK, COLS), BF16),
                pltpu.VMEM((OWN, HOPS + 1, 2, BLK, HD), F32),
                pair, pair, pair, pair, pair, pair,
                dma((HOPS, OWN)), dma((HOPS, OWN)),
                pair, pair, pair, pair, pair, pair,
                dma((HOPS, OWN)), dma((HOPS, OWN)),
                pair, pair,
                dma((len(stages), most)), dma((len(stages), most)),
            ],
            compiler_params=pltpu.CompilerParams(
                collective_id=0, has_side_effects=True, vmem_limit_bytes=60 * 1024 * 1024
            ),
        )(queries[0], key_states[0], value_states[0], cotangent[0], aux, core_central)
        core = jnp.transpose(core[:J1].reshape(J1, BOND, HQ), (2, 0, 1))
        core = core / jnp.sqrt(jnp.float32(all_tokens * HD))
        return dq[None], dk[None], dv[None], core

    return jax.shard_map(
        step,
        mesh=mesh,
        in_specs=(P("dp", "ctx", None),) * 4 + (P(), P()),
        out_specs=(P("dp", "ctx", None),) * 3 + (P(),),
        check_vma=False,
    )
```

```python
import functools
import math

import jax
import jax.numpy as jnp
from jax import lax
from jax.experimental import pallas as pl
from jax.experimental.pallas import tpu as pltpu
from jax.sharding import PartitionSpec as P

HD = 128
HQ = 16
HK = 8
J1 = 42
JP = 48
BOND = 8
WINDOW = 1024
TOK = 128
BLK = 2 * TOK
OWN = HK // 2
HOPS = WINDOW // BLK
COLS = 2 * BLK
SCORE_SCALE = 168.0 ** (-0.5)
EXP_SCALE = SCORE_SCALE * math.log2(math.e)
MASK_FILL = -1e30
F32 = jnp.float32
BF16 = jnp.bfloat16
MESH = pl.DeviceIdType.MESH

FIRST = [
    "e", "e", "e", "e", ("f", 1, 0, 0), "e", "e", "e", ("f", 1, 0, 1), "e", "e", "e", ("f", 1, 1, 0), "e",
    "e", "e", "e", ("f", 2, 0, 0), "e", "e", "d", ("f", 2, 0, 1), ("f", 1, 1, 1), ("f", 3, 0, 0),
    ("f", 3, 0, 1), ("f", 2, 1, 0), ("f", 4, 0, 0), ("f", 4, 0, 1), ("f", 2, 1, 1), ("f", 3, 1, 0),
]
HOOKS = {
    (0, "b"): [("f", 1, 2, 0)],
    (0, "e"): [("f", 3, 1, 1)],
    (0, "f"): [("b", 0, 0, 1)],
    (0, "g"): [("f", 4, 1, 0)],
    (0, "h"): [("f", 1, 2, 1), ("b", 0, 0, 0), ("f", 4, 1, 1), ("b", 1, 0, 1), ("f", 2, 2, 0)],
    (1, "b"): [("b", 1, 0, 0), ("f", 2, 2, 1)],
    (1, "c"): [("f", 1, 3, 0)],
    (1, "d"): [("b", 2, 0, 1)],
    (1, "f"): [("f", 3, 2, 0)],
    (1, "g"): [("b", 0, 1, 1), ("f", 3, 2, 1)],
    (1, "h"): [("b", 0, 1, 0), ("f", 1, 3, 1), ("b", 2, 0, 0), ("f", 4, 2, 0), ("b", 1, 1, 1), ("f", 4, 2, 1), ("b", 1, 1, 0), ("f", 2, 3, 0), ("b", 3, 0, 1), ("f", 2, 3, 1)],
    (2, "b"): [("b", 2, 1, 1)],
    (2, "d"): [("b", 2, 1, 0)],
    (2, "e"): [("f", 3, 3, 0)],
    (2, "g"): [("f", 3, 3, 1), ("b", 0, 2, 1), ("b", 3, 0, 0), ("b", 4, 0, 1)],
    (2, "h"): [("f", 4, 3, 0), ("b", 0, 2, 0), ("f", 4, 3, 1), ("b", 1, 2, 1), ("b", 3, 1, 1), ("b", 3, 1, 0), ("b", 4, 0, 0)],
    (3, "c"): [("b", 1, 2, 0)],
    (3, "f"): [("b", 0, 3, 1), ("b", 2, 2, 1), ("b", 4, 1, 1)],
    (3, "g"): [("b", 4, 1, 0)],
}
LAST = [
    "f", ("b", 0, 3, 0), "f", "f", ("b", 1, 3, 1), "f", "g", ("b", 2, 2, 0), "g", "g", ("b", 1, 3, 0), "g",
    "g", ("b", 2, 3, 1), "g", "g", ("b", 3, 2, 1), "g", ("a", 0), ("b", 2, 3, 0), ("b", 3, 2, 0), ("a", 1),
    ("b", 3, 3, 1), ("b", 4, 2, 1), ("b", 3, 3, 0), ("b", 4, 2, 0), ("a", 2), ("b", 4, 3, 1), ("b", 4, 3, 0),
    ("a", 3),
]


def reduce_stages(mesh_shape):
    dp, ctx = mesh_shape["dp"], mesh_shape["ctx"]
    near = min(4, dp)
    stages = [(0, near, 0, 2), (2, dp // near, 0, 1)]
    rest, bit = ctx // 2, 1
    while rest > 1:
        size = min(4, rest)
        stages.append((0, 1, bit, size))
        rest, bit = rest // size, bit + 2
    return [stage for stage in stages if stage[1] * stage[3] > 1]


def nt(a, b):
    return lax.dot_general(a, b, (((1,), (1,)), ((), ())), preferred_element_type=F32)


def nn(a, b):
    return lax.dot_general(a, b, (((1,), (0,)), ((), ())), preferred_element_type=F32)


def lanes(start):
    return pl.ds(pl.multiple_of(start * HD, HD), HD)


def rows(start):
    return pl.ds(pl.multiple_of(start * TOK, TOK), TOK)


def kernel(
    n_ctx, stages,
    q_ref, k_ref, v_ref, cot_ref, aux_ref, cen_ref,
    dq_ref, dk_ref, dv_ref, core_ref,
    kv, qbuf, dabuf, dasend, atx, atin, dqx, csend, crecv, finx, arbuf,
    cots, est, mat, cent, cenw, kt, vt, dat, sc, ph, ds, part,
    kx_s, kx_r, loc, qx_s, qx_r, qloc, hop_s, hop_r, da_s, da_r, at_s, at_r,
    dq_s, dq_r, ch_s, ch_r, fin_s, fin_r, ar_s, ar_r,
):
    me_dp = lax.axis_index("dp")
    me = lax.axis_index("ctx")
    zpos = me // 2
    xlo = lax.rem(me, 2)
    other = 1 - xlo
    partner = {"ctx": me + 1 - 2 * xlo}
    up = {"ctx": lax.rem(me + 2, n_ctx)}
    down = {"ctx": lax.rem(me + n_ctx - 2, n_ctx)}

    def stage_peers(stage):
        dp_bit, dp_size, ctx_bit, ctx_size = stage
        size = dp_size * ctx_size
        dp_pos = lax.rem(me_dp // (1 << dp_bit), dp_size)
        ctx_pos = lax.rem(me // (1 << ctx_bit), ctx_size)
        pos = dp_pos * ctx_size + ctx_pos
        out = []
        for d in range(1, size):
            their = lax.rem(pos + d, size)
            dev = {
                "dp": me_dp + (their // ctx_size - dp_pos) * (1 << dp_bit),
                "ctx": me + (lax.rem(their, ctx_size) - ctx_pos) * (1 << ctx_bit),
            }
            out.append((d, dev))
        return pos, out

    def remote(src, dst, s, r, dev):
        return pltpu.make_async_remote_copy(
            src_ref=src, dst_ref=dst, send_sem=s, recv_sem=r, device_id=dev, device_id_type=MESH
        )

    barrier = pltpu.get_barrier_semaphore()
    greet = [partner, up, down]
    for stage in stages:
        greet += [dev for _, dev in stage_peers(stage)[1]]
    for dev in greet:
        pl.semaphore_signal(barrier, inc=1, device_id=dev, device_id_type=MESH)
    pl.semaphore_wait(barrier, len(greet))

    srcs = (k_ref, v_ref)

    def kx(h, c):
        return remote(
            srcs[c].at[:, lanes(other * OWN + h)], kv.at[0, h, c, rows(xlo)],
            kx_s.at[h, c], kx_r.at[h, c], partner,
        )

    def kloc(h, c):
        return pltpu.make_async_copy(
            srcs[c].at[:, lanes(xlo * OWN + h)], kv.at[0, h, c, rows(xlo)], loc.at[h, c]
        )

    def qx(h, g):
        return remote(
            q_ref.at[:, lanes(other * 2 * OWN + 2 * h + g)], qbuf.at[h, rows(2 * g + xlo)],
            qx_s.at[h, g], qx_r.at[h, g], partner,
        )

    def qlocal(h, g):
        return pltpu.make_async_copy(
            q_ref.at[:, lanes(xlo * 2 * OWN + 2 * h + g)], qbuf.at[h, rows(2 * g + xlo)], qloc.at[h, g]
        )

    def hop(s, h, c):
        return remote(kv.at[s - 1, h, c], kv.at[s, h, c], hop_s.at[s - 1, h, c], hop_r.at[s - 1, h, c], up)

    def dax(h, g):
        return remote(
            dasend.at[h, g], dabuf.at[h, rows(2 * g + xlo)], da_s.at[h, g], da_r.at[h, g], partner
        )

    def attnx(h, g):
        return remote(
            atx.at[h, rows(2 * g + other)], atin.at[h, g], at_s.at[h, g], at_r.at[h, g], partner
        )

    def dqxc(h, g):
        return remote(
            dqx.at[h, rows(2 * g + other)], dq_ref.at[:, lanes(xlo * 2 * OWN + 2 * h + g)],
            dq_s.at[h, g], dq_r.at[h, g], partner,
        )

    def chain(st, h, c):
        return remote(
            csend.at[st, h, c], crecv.at[st, h, c], ch_s.at[st, h, c], ch_r.at[st, h, c], down
        )

    outs = (dk_ref, dv_ref)

    def finc(h, c):
        return remote(
            finx.at[h, c], outs[c].at[:, lanes(xlo * OWN + h)], fin_s.at[h, c], fin_r.at[h, c], partner
        )

    for h in range(OWN):
        for c in range(2):
            kx(h, c).start()
            kloc(h, c).start()
    for h in range(OWN):
        for c in range(2):
            qx(h, c).start()
            qlocal(h, c).start()

    @pl.loop(0, TOK)
    def _(t):
        cots[pl.ds(t * JP + JP - 8, 8), :] = jnp.zeros((8, HD), F32)

    @pl.loop(0, J1)
    def _(j):
        cots[pl.ds(j, TOK, stride=JP), :] = cot_ref[:, lanes(j)].astype(F32)

    @pl.loop(0, BOND)
    def _(b):
        cent[rows(b), :] = cen_ref[b].T
        cenw[:, lanes(b)] = cen_ref[b]

    def cot_tok(t):
        return cots[pl.ds(pl.multiple_of(t * JP, JP), JP), :].astype(BF16)

    def e_terms(t):
        e = nn(aux_ref[...], jnp.concatenate([cot_tok(t), cot_tok(t + 1)], axis=1)).astype(BF16)
        for u in range(2):
            r16 = pl.ds(pl.multiple_of((t + u) * HQ, HQ), HQ)
            for b in range(BOND):
                est[r16, b * HD : (b + 1) * HD] = e[b * HQ : (b + 1) * HQ, u * HD : (u + 1) * HD]

    def forward(s, h, c):
        if s == 1:
            kx(h, c).wait_recv()
            kloc(h, c).wait()
        else:
            hop(s - 1, h, c).wait_recv()
        hop(s, h, c).start()

    def d_terms():
        @pl.loop(0, 8)
        def _(n):
            rr = pl.ds(pl.multiple_of(n * 256, 256), 256)
            mat[rr, :] = nn(est[rr, :], cent[...]).astype(BF16).astype(F32)

        for h in range(OWN):
            for g in range(2):
                i_other = other * 2 * OWN + 2 * h + g
                dasend[h, g] = mat[pl.ds(i_other, TOK, stride=HQ), :].astype(BF16)
        for h in range(OWN):
            for g in range(2):
                dax(h, g).start()
        for h in range(OWN):
            for g in range(2):
                i_own = xlo * 2 * OWN + 2 * h + g
                dabuf[h, rows(2 * g + xlo)] = mat[pl.ds(i_own, TOK, stride=HQ), :].astype(BF16)

    pieces = TOK // FIRST.count("e")
    done = 0
    for item in FIRST:
        if item == "e":

            @pl.loop(done // 2, (done + pieces) // 2, unroll=4)
            def _(n):
                e_terms(2 * n)

            done += pieces
        elif item == "d":
            d_terms()
        else:
            forward(*item[1:])

    t_pos = lax.rem(lax.broadcasted_iota(jnp.int32, (TOK, COLS), 1), BLK)
    r_iota = lax.broadcasted_iota(jnp.int32, (TOK, COLS), 0)

    def back(st, hh, c):
        total = part[hh, HOPS - st, c]
        if st > 0:
            chain(st - 1, hh, c).wait_recv()
            total = crecv[st - 1, hh, c].astype(F32) + total
        total = total.astype(BF16)
        if st < HOPS:
            csend[st, hh, c] = total
            chain(st, hh, c).start()
        else:
            part[hh, 0, c] = total.astype(F32)
            finx[hh, c] = part[hh, 0, c, rows(other)].astype(BF16)
            finc(hh, c).start()
            outs[c][:, lanes(xlo * OWN + hh)] = part[hh, 0, c, rows(xlo)].astype(BF16)

    def hook(h, name):
        for (n, point), todo in HOOKS.items():
            if point == name:

                @pl.when(h == n)
                def _():
                    for item in todo:
                        if item[0] == "f":
                            forward(*item[1:])
                        else:
                            back(*item[1:])

    @pl.loop(0, OWN)
    def _(h):
        for g in range(2):
            qx(h, g).wait_recv()
            qlocal(h, g).wait()
        hop(HOPS, h, 0).wait_recv()
        qh = qbuf[h]
        hook(h, "a")

        def scores(s, u):
            return nt(kv[s, h, 0, rows(u)], qh)

        m = jnp.full((1, COLS), MASK_FILL, F32)
        for u in range(2):
            causal = t_pos >= r_iota + u * TOK
            far = jnp.where(zpos >= HOPS, scores(HOPS, u), MASK_FILL)
            x = jnp.where(causal, scores(0, u), far)
            sc[u * TOK : (u + 1) * TOK, :] = x
            m = jnp.maximum(m, jnp.max(x, axis=0, keepdims=True))

        def score_step(w, m):
            s = w // 2
            x = jnp.where(zpos >= s, scores(s, lax.rem(w, 2)), MASK_FILL)
            sc[rows(w), :] = x
            return jnp.maximum(m, jnp.max(x, axis=0, keepdims=True))

        m = lax.fori_loop(2, 2 * HOPS, score_step, m)

        hook(h, "b")

        def exp_step(w, l):
            e = jnp.exp2((sc[rows(w), :] - m) * EXP_SCALE)
            sc[rows(w), :] = e
            return l + jnp.sum(e, axis=0, keepdims=True)

        l = lax.fori_loop(0, 2 * HOPS, exp_step, jnp.zeros((1, COLS), F32))
        inv = 1.0 / l
        hook(h, "c")
        hop(HOPS, h, 1).wait_recv()
        for s in range(HOPS + 1):
            for u in range(2):
                w = 2 * s + u
                vt[:, w * TOK : (w + 1) * TOK] = kv[s, h, 1, u * TOK : (u + 1) * TOK].T

        for u in range(2):
            causal = t_pos >= r_iota + u * TOK
            p = sc[u * TOK : (u + 1) * TOK, :] * inv
            sc[u * TOK : (u + 1) * TOK, :] = p
            ph[u * TOK : (u + 1) * TOK, :] = jnp.where(causal, p, 0.0).astype(BF16)
            w = 2 * HOPS + u
            ph[w * TOK : (w + 1) * TOK, :] = jnp.where(causal, 0.0, p).astype(BF16)

        @pl.loop(2, 2 * HOPS)
        def _(w):
            p = sc[rows(w), :] * inv
            sc[rows(w), :] = p
            ph[rows(w), :] = p.astype(BF16)

        hook(h, "d")
        for g in range(2):
            dax(h, g).wait_recv()
        dah = dabuf[h]
        dat[...] = dah.T
        att = nn(vt[...], ph[...]).astype(BF16)
        delta = jnp.sum(att.astype(F32) * dat[...].astype(F32), axis=0, keepdims=True)
        atx[h] = att.T
        for g in range(2):
            attnx(h, g).start()
        hook(h, "e")

        @pl.loop(0, HOPS + 1)
        def _(s):
            for u in range(2):
                part[h, s, 1, u * TOK : (u + 1) * TOK] = nn(ph[rows(2 * s + u), :], dah)

        hook(h, "f")

        def dprob(s, u):
            return nn(kv[s, h, 1, rows(u)], dat[...])

        for u in range(2):
            causal = t_pos >= r_iota + u * TOK
            dp = jnp.where(causal, dprob(0, u), dprob(HOPS, u))
            d = sc[u * TOK : (u + 1) * TOK, :] * (dp - delta)
            ds[u * TOK : (u + 1) * TOK, :] = jnp.where(causal, d, 0.0).astype(BF16)
            w = 2 * HOPS + u
            ds[w * TOK : (w + 1) * TOK, :] = jnp.where(causal, 0.0, d).astype(BF16)

        @pl.loop(2, 2 * HOPS)
        def _(w):
            dp = dprob(w // 2, lax.rem(w, 2))
            ds[rows(w), :] = (sc[rows(w), :] * (dp - delta)).astype(BF16)

        hook(h, "g")
        for s in range(HOPS + 1):
            for u in range(2):
                w = 2 * s + u
                kt[:, w * TOK : (w + 1) * TOK] = kv[s, h, 0, u * TOK : (u + 1) * TOK].T
        dqt = (nn(kt[...], ds[...]) * SCORE_SCALE).astype(BF16)
        dqx[h] = dqt.T
        for g in range(2):
            dqxc(h, g).start()
        for g in range(2):
            dq_ref[:, lanes(xlo * 2 * OWN + 2 * h + g)] = dqx[h, rows(2 * g + xlo)]

        @pl.loop(0, HOPS + 1)
        def _(s):
            for u in range(2):
                part[h, s, 0, u * TOK : (u + 1) * TOK] = nn(ds[rows(2 * s + u), :], qh) * SCORE_SCALE

        hook(h, "h")

    def attn_terms():
        for h in range(OWN):
            for g in range(2):
                i_own = xlo * 2 * OWN + 2 * h + g
                mat[pl.ds(i_own, TOK, stride=HQ), :] = atx[h, rows(2 * g + xlo)].astype(F32)
        for h in range(OWN):
            for g in range(2):
                attnx(h, g).wait_recv()
                i_other = other * 2 * OWN + 2 * h + g
                mat[pl.ds(i_other, TOK, stride=HQ), :] = atin[h, g].astype(F32)

    def f_terms(lo, hi):
        @pl.loop(lo, hi)
        def _(n):
            rr = pl.ds(pl.multiple_of(n * 256, 256), 256)
            est[rr, :] = nn(mat[rr, :].astype(BF16), cenw[...]).astype(BF16)

    def core_step(n, acc):
        def f_tok(t):
            r16 = pl.ds(pl.multiple_of(t * HQ, HQ), HQ)
            return jnp.concatenate([est[r16, b * HD : (b + 1) * HD] for b in range(BOND)], axis=0)

        cot2 = jnp.concatenate([cot_tok(2 * n), cot_tok(2 * n + 1)], axis=1)
        return acc + nt(cot2, jnp.concatenate([f_tok(2 * n), f_tok(2 * n + 1)], axis=1))

    def reduce_copy(k, d, dev):
        pos = stage_peers(stages[k])[0]
        return remote(arbuf.at[k, pos], arbuf.at[k, pos], ar_s.at[k, d], ar_r.at[k, d], dev)

    def reduce_start(k):
        pos, peers = stage_peers(stages[k])
        arbuf[k, pos] = core_ref[...]
        for d, dev in peers:
            reduce_copy(k, d, dev).start()

    def reduce_end(k):
        for d, dev in stage_peers(stages[k])[1]:
            reduce_copy(k, d, dev).wait_recv()
        total = arbuf[k, 0]
        for n in range(1, stages[k][1] * stages[k][3]):
            total = total + arbuf[k, n]
        core_ref[...] = total
        for d, dev in stage_peers(stages[k])[1]:
            reduce_copy(k, d, dev).wait_send()

    core_ref[...] = jnp.zeros((JP, BOND * HQ), F32)
    n_f = LAST.count("f")
    n_g = LAST.count("g")
    f_done = g_done = 0
    reduced = -1
    for item in LAST:
        if item == "f":
            if f_done == 0:
                attn_terms()
            f_terms(f_done * 8 // n_f, (f_done + 1) * 8 // n_f)
            f_done += 1
        elif item == "g":
            lo, hi = g_done * TOK // 2 // n_g, (g_done + 1) * TOK // 2 // n_g
            core_ref[...] = lax.fori_loop(lo, hi, core_step, core_ref[...], unroll=4)
            g_done += 1
        elif item[0] == "b":
            back(*item[1:])
        elif item[1] < len(stages):
            if reduced >= 0:
                reduce_end(reduced)
            reduced = item[1]
            reduce_start(reduced)
    reduce_end(reduced)

    for h in range(OWN):
        for c in range(2):
            kx(h, c).wait_send()
            qx(h, c).wait_send()
            dax(h, c).wait_send()
            attnx(h, c).wait_send()
            dqxc(h, c).wait()
            finc(h, c).wait()
            for s in range(HOPS):
                hop(s + 1, h, c).wait_send()
                chain(s, h, c).wait_send()


def solution(mesh):
    n_ctx = mesh.shape["ctx"]
    stages = reduce_stages(mesh.shape)
    all_tokens = TOK * n_ctx * mesh.shape["dp"]

    def step(queries, key_states, value_states, cotangent, core_aux, core_central):
        aux = jnp.transpose(core_aux, (2, 0, 1)).reshape(BOND * HQ, J1)
        aux = jnp.pad(aux, ((0, 0), (0, JP - J1)))
        vm = pl.BlockSpec(memory_space=pltpu.VMEM)
        dma = pltpu.SemaphoreType.DMA
        pair = dma((OWN, 2))
        width = 2 * OWN * HD
        most = max(stage[1] * stage[3] for stage in stages)
        dq, dk, dv, core = pl.pallas_call(
            functools.partial(kernel, n_ctx, stages),
            out_shape=(
                jax.ShapeDtypeStruct((TOK, HQ * HD), BF16),
                jax.ShapeDtypeStruct((TOK, HK * HD), BF16),
                jax.ShapeDtypeStruct((TOK, HK * HD), BF16),
                jax.ShapeDtypeStruct((JP, BOND * HQ), F32),
            ),
            in_specs=[vm] * 6,
            out_specs=(vm, vm, vm, vm),
            scratch_shapes=[
                pltpu.VMEM((HOPS + 1, OWN, 2, BLK, HD), BF16),
                pltpu.VMEM((OWN, COLS, HD), BF16),
                pltpu.VMEM((OWN, COLS, HD), BF16),
                pltpu.VMEM((OWN, 2, TOK, HD), BF16),
                pltpu.VMEM((OWN, COLS, HD), BF16),
                pltpu.VMEM((OWN, 2, TOK, HD), BF16),
                pltpu.VMEM((OWN, COLS, HD), BF16),
                pltpu.VMEM((HOPS, OWN, 2, BLK, HD), BF16),
                pltpu.VMEM((HOPS, OWN, 2, BLK, HD), BF16),
                pltpu.VMEM((OWN, 2, TOK, HD), BF16),
                pltpu.VMEM((len(stages), most, JP, BOND * HQ), F32),
                pltpu.VMEM((TOK * JP, HD), F32),
                pltpu.VMEM((TOK * HQ, BOND * HD), BF16),
                pltpu.VMEM((TOK * HQ, HD), F32),
                pltpu.VMEM((BOND * HD, HD), BF16),
                pltpu.VMEM((HD, BOND * HD), BF16),
                pltpu.VMEM((HD, (HOPS + 1) * BLK), BF16),
                pltpu.VMEM((HD, (HOPS + 1) * BLK), BF16),
                pltpu.VMEM((HD, COLS), BF16),
                pltpu.VMEM((HOPS * BLK, COLS), F32),
                pltpu.VMEM(((HOPS + 1) * BLK, COLS), BF16),
                pltpu.VMEM(((HOPS + 1) * BLK, COLS), BF16),
                pltpu.VMEM((OWN, HOPS + 1, 2, BLK, HD), F32),
                pair, pair, pair, pair, pair, pair,
                dma((HOPS, OWN, 2)), dma((HOPS, OWN, 2)),
                pair, pair, pair, pair, pair, pair,
                dma((HOPS, OWN, 2)), dma((HOPS, OWN, 2)),
                pair, pair,
                dma((len(stages), most)), dma((len(stages), most)),
            ],
            compiler_params=pltpu.CompilerParams(
                collective_id=0, has_side_effects=True, vmem_limit_bytes=60 * 1024 * 1024
            ),
        )(queries[0], key_states[0], value_states[0], cotangent[0], aux, core_central)
        core = jnp.transpose(core[:J1].reshape(J1, BOND, HQ), (2, 0, 1))
        core = core / jnp.sqrt(jnp.float32(all_tokens * HD))
        return dq[None], dk[None], dv[None], core

    return jax.shard_map(
        step,
        mesh=mesh,
        in_specs=(P("dp", "ctx", None),) * 4 + (P(), P()),
        out_specs=(P("dp", "ctx", None),) * 3 + (P(),),
        check_vma=False,
    )
```

```python
import functools
import math

import jax
import jax.numpy as jnp
from jax import lax
from jax.experimental import pallas as pl
from jax.experimental.pallas import tpu as pltpu
from jax.sharding import PartitionSpec as P

HD = 128
HQ = 16
HK = 8
J1 = 42
JP = 48
BOND = 8
WINDOW = 1024
TOK = 128
BLK = 2 * TOK
OWN = HK // 2
HOPS = WINDOW // BLK
COLS = 2 * BLK
SCORE_SCALE = 168.0 ** (-0.5)
EXP_SCALE = SCORE_SCALE * math.log2(math.e)
MASK_FILL = -1e30
F32 = jnp.float32
BF16 = jnp.bfloat16
MESH = pl.DeviceIdType.MESH
SPLIT = 2
PIECES_A = 2
PIECES_G = 4

FIRST = [
    "e", "e", "e", "e", ("f", 1, 0, 0), ("f", 1, 0, 1), ("f", 1, 1, 0), ("f", 1, 1, 1), ("f", 1, 2, 0),
    ("f", 2, 0, 0), "e", "e", ("f", 2, 0, 1), "e", ("f", 2, 1, 0), "e", "e", ("f", 3, 0, 0), "e",
    ("f", 3, 0, 1), "e", "e", ("f", 2, 1, 1), "e", "e", "e", ("f", 4, 0, 0), "e", ("f", 4, 0, 1),
    ("f", 3, 1, 0), "d", ("f", 3, 1, 1), ("f", 1, 2, 1),
]
HOOKS = {
    (0, "e"): [("f", 4, 1, 0)],
    (0, "f"): [("b", 0, 0, 1)],
    (0, "g"): [("f", 4, 1, 1)],
    (0, "h"): [("b", 0, 0, 0), ("f", 2, 2, 0), ("f", 2, 2, 1), ("f", 1, 3, 0)],
    (1, "b"): [("b", 1, 0, 1)],
    (1, "c"): [("f", 1, 3, 1)],
    (1, "d"): [("b", 1, 0, 0)],
    (1, "e"): [("f", 3, 2, 0)],
    (1, "f"): [("b", 0, 1, 1)],
    (1, "g"): [("b", 2, 0, 1), ("f", 3, 2, 1), ("f", 2, 3, 0)],
    (1, "h"): [("b", 0, 1, 0), ("b", 1, 1, 1), ("f", 4, 2, 0), ("f", 2, 3, 1), ("A", 0, 0), ("b", 2, 0, 0), ("A", 0, 1), ("f", 4, 2, 1), ("G", 0, 0), ("b", 1, 1, 0), ("b", 3, 0, 1), ("G", 0, 1), ("f", 3, 3, 0)],
    (2, "a"): [("b", 2, 1, 1)],
    (2, "b"): [("b", 3, 0, 0), ("f", 3, 3, 1)],
    (2, "e"): [("b", 2, 1, 0), ("f", 4, 3, 0)],
    (2, "f"): [("b", 0, 2, 1)],
    (2, "g"): [("b", 3, 1, 1), ("f", 4, 3, 1)],
    (2, "h"): [("b", 0, 2, 0)],
    (3, "b"): [("b", 3, 1, 0), ("b", 1, 2, 1)],
    (3, "f"): [("b", 0, 3, 1)],
    (3, "g"): [("b", 1, 2, 0)],
}
LAST = [
    ("b", 0, 3, 0), ("b", 2, 2, 1), ("G", 0, 2), ("G", 0, 3), ("b", 1, 3, 1), ("A", 1, 0), ("b", 4, 0, 0),
    ("A", 1, 1), ("b", 2, 2, 0), ("G", 1, 0), ("G", 1, 1), ("b", 1, 3, 0), ("G", 1, 2), ("b", 3, 2, 1),
    ("G", 1, 3), ("b", 2, 3, 1), ("a", 0), ("b", 2, 3, 0), ("a", 1), ("b", 3, 2, 0), ("b", 4, 2, 1),
    ("b", 4, 0, 1), ("b", 4, 1, 0), ("b", 3, 3, 1), ("a", 2), ("b", 3, 3, 0), ("b", 4, 2, 0), ("b", 4, 1, 1),
    ("b", 4, 3, 1), ("b", 4, 3, 0), ("a", 3),
]


def reduce_stages(mesh_shape):
    dp, ctx = mesh_shape["dp"], mesh_shape["ctx"]
    near = min(4, dp)
    stages = [(0, near, 0, 2), (2, dp // near, 0, 1)]
    rest, bit = ctx // 2, 1
    while rest > 1:
        size = min(4, rest)
        stages.append((0, 1, bit, size))
        rest, bit = rest // size, bit + 2
    return [stage for stage in stages if stage[1] * stage[3] > 1]


def nt(a, b):
    return lax.dot_general(a, b, (((1,), (1,)), ((), ())), preferred_element_type=F32)


def nn(a, b):
    return lax.dot_general(a, b, (((1,), (0,)), ((), ())), preferred_element_type=F32)


def lanes(start):
    return pl.ds(pl.multiple_of(start * HD, HD), HD)


def rows(start):
    return pl.ds(pl.multiple_of(start * TOK, TOK), TOK)


def kernel(
    n_ctx, stages,
    q_ref, k_ref, v_ref, cot_ref, aux_ref, cen_ref,
    dq_ref, dk_ref, dv_ref, core_ref,
    kv, qbuf, dabuf, dasend, atx, atin, dqx, csend, crecv, finx, arbuf,
    aux, cots, est, fst, gacc, mat, cent, cenw, kt, vt, dat, sc, ph, ds, part,
    kx_s, kx_r, loc, qx_s, qx_r, qloc, hop_s, hop_r, da_s, da_r, at_s, at_r,
    dq_s, dq_r, ch_s, ch_r, fin_s, fin_r, ar_s, ar_r, own_s, own_r,
):
    me_dp = lax.axis_index("dp")
    me = lax.axis_index("ctx")
    zpos = me // 2
    xlo = lax.rem(me, 2)
    other = 1 - xlo
    partner = {"ctx": me + 1 - 2 * xlo}
    up = {"ctx": lax.rem(me + 2, n_ctx)}
    down = {"ctx": lax.rem(me + n_ctx - 2, n_ctx)}

    def stage_peers(stage):
        dp_bit, dp_size, ctx_bit, ctx_size = stage
        size = dp_size * ctx_size
        dp_pos = lax.rem(me_dp // (1 << dp_bit), dp_size)
        ctx_pos = lax.rem(me // (1 << ctx_bit), ctx_size)
        pos = dp_pos * ctx_size + ctx_pos
        out = []
        for d in range(1, size):
            their = lax.rem(pos + d, size)
            dev = {
                "dp": me_dp + (their // ctx_size - dp_pos) * (1 << dp_bit),
                "ctx": me + (lax.rem(their, ctx_size) - ctx_pos) * (1 << ctx_bit),
            }
            out.append((d, dev))
        return pos, out

    def remote(src, dst, s, r, dev):
        return pltpu.make_async_remote_copy(
            src_ref=src, dst_ref=dst, send_sem=s, recv_sem=r, device_id=dev, device_id_type=MESH
        )

    barrier = pltpu.get_barrier_semaphore()
    greet = [partner, up, down]
    for stage in (stage for stage in stages if stage[2] == 0):
        greet += [dev for _, dev in stage_peers(stage)[1]]
    for dev in greet:
        pl.semaphore_signal(barrier, inc=1, device_id=dev, device_id_type=MESH)
    pl.semaphore_wait(barrier, len(greet))

    srcs = (k_ref, v_ref)

    def kx(h, c):
        return remote(
            srcs[c].at[:, lanes(other * OWN + h)], kv.at[0, h, c, rows(xlo)],
            kx_s.at[h, c], kx_r.at[h, c], partner,
        )

    def kloc(h, c):
        return pltpu.make_async_copy(
            srcs[c].at[:, lanes(xlo * OWN + h)], kv.at[0, h, c, rows(xlo)], loc.at[h, c]
        )

    def qx(h, g):
        return remote(
            q_ref.at[:, lanes(other * 2 * OWN + 2 * h + g)], qbuf.at[h, rows(2 * g + xlo)],
            qx_s.at[h, g], qx_r.at[h, g], partner,
        )

    def qlocal(h, g):
        return pltpu.make_async_copy(
            q_ref.at[:, lanes(xlo * 2 * OWN + 2 * h + g)], qbuf.at[h, rows(2 * g + xlo)], qloc.at[h, g]
        )

    def own(h, c):
        return remote(
            srcs[c].at[:, lanes(xlo * OWN + h)], kv.at[1, h, c, rows(xlo)],
            own_s.at[h, c], own_r.at[h, c], up,
        )

    def rest(h, c):
        return remote(
            kv.at[0, h, c, rows(other)], kv.at[1, h, c, rows(other)],
            hop_s.at[0, h, c], hop_r.at[0, h, c], up,
        )

    def hop(s, h, c):
        return remote(kv.at[s - 1, h, c], kv.at[s, h, c], hop_s.at[s - 1, h, c], hop_r.at[s - 1, h, c], up)

    def dax(h, g):
        return remote(
            dasend.at[h, g], dabuf.at[h, rows(2 * g + xlo)], da_s.at[h, g], da_r.at[h, g], partner
        )

    def attnx(h, g):
        return remote(
            atx.at[h, rows(2 * g + other)], atin.at[h, g], at_s.at[h, g], at_r.at[h, g], partner
        )

    def dqxc(h, g):
        return remote(
            dqx.at[h, rows(2 * g + other)], dq_ref.at[:, lanes(xlo * 2 * OWN + 2 * h + g)],
            dq_s.at[h, g], dq_r.at[h, g], partner,
        )

    def chain(st, h, c):
        return remote(
            csend.at[st, h, c], crecv.at[st, h, c], ch_s.at[st, h, c], ch_r.at[st, h, c], down
        )

    outs = (dk_ref, dv_ref)

    def finc(h, c):
        return remote(
            finx.at[h, c], outs[c].at[:, lanes(xlo * OWN + h)], fin_s.at[h, c], fin_r.at[h, c], partner
        )

    for h in range(OWN):
        for c in range(2):
            kx(h, c).start()
            kloc(h, c).start()
            if h < SPLIT:
                own(h, c).start()
    for h in range(OWN):
        for c in range(2):
            qx(h, c).start()
            qlocal(h, c).start()

    aux[...] = jnp.zeros(aux.shape, BF16)
    aux[:, :J1] = aux_ref[...]
    gacc[...] = jnp.zeros(gacc.shape, F32)

    @pl.loop(0, TOK)
    def _(t):
        cots[pl.ds(t * JP + JP - 8, 8), :] = jnp.zeros((8, HD), F32)

    @pl.loop(0, J1)
    def _(j):
        cots[pl.ds(j, TOK, stride=JP), :] = cot_ref[:, lanes(j)].astype(F32)

    @pl.loop(0, BOND)
    def _(b):
        cent[rows(b), :] = cen_ref[b].T
        cenw[:, lanes(b)] = cen_ref[b]

    def cot_tok(t):
        return cots[pl.ds(pl.multiple_of(t * JP, JP), JP), :].astype(BF16)

    def e_terms(t):
        e = nn(aux[...], jnp.concatenate([cot_tok(t), cot_tok(t + 1)], axis=1)).astype(BF16)
        for u in range(2):
            r16 = pl.ds(pl.multiple_of((t + u) * HQ, HQ), HQ)
            for b in range(BOND):
                est[r16, b * HD : (b + 1) * HD] = e[b * HQ : (b + 1) * HQ, u * HD : (u + 1) * HD]

    def forward(s, h, c):
        if s == 1:
            kx(h, c).wait_recv()
            kloc(h, c).wait()
        elif s == 2 and h < SPLIT:
            own(h, c).wait_recv()
            rest(h, c).wait_recv()
        else:
            hop(s - 1, h, c).wait_recv()
        if s == 1 and h < SPLIT:
            rest(h, c).start()
        else:
            hop(s, h, c).start()

    def d_terms():
        @pl.loop(0, 8)
        def _(n):
            rr = pl.ds(pl.multiple_of(n * 256, 256), 256)
            mat[rr, :] = nn(est[rr, :], cent[...]).astype(BF16).astype(F32)

        for h in range(OWN):
            for g in range(2):
                i_other = other * 2 * OWN + 2 * h + g
                dasend[h, g] = mat[pl.ds(i_other, TOK, stride=HQ), :].astype(BF16)
        for h in range(OWN):
            for g in range(2):
                dax(h, g).start()
        for h in range(OWN):
            for g in range(2):
                i_own = xlo * 2 * OWN + 2 * h + g
                dabuf[h, rows(2 * g + xlo)] = mat[pl.ds(i_own, TOK, stride=HQ), :].astype(BF16)

    pieces = TOK // FIRST.count("e")
    done = 0
    for item in FIRST:
        if item == "e":

            @pl.loop(done // 2, (done + pieces) // 2, unroll=4)
            def _(n):
                e_terms(2 * n)

            done += pieces
        elif item == "d":
            d_terms()
        else:
            forward(*item[1:])

    t_pos = lax.rem(lax.broadcasted_iota(jnp.int32, (TOK, COLS), 1), BLK)
    r_iota = lax.broadcasted_iota(jnp.int32, (TOK, COLS), 0)

    def back(st, hh, c):
        total = part[hh, HOPS - st, c]
        if st > 0:
            chain(st - 1, hh, c).wait_recv()
            total = crecv[st - 1, hh, c].astype(F32) + total
        total = total.astype(BF16)
        if st < HOPS:
            csend[st, hh, c] = total
            chain(st, hh, c).start()
        else:
            part[hh, 0, c] = total.astype(F32)
            finx[hh, c] = part[hh, 0, c, rows(other)].astype(BF16)
            finc(hh, c).start()
            outs[c][:, lanes(xlo * OWN + hh)] = part[hh, 0, c, rows(xlo)].astype(BF16)

    def attn_terms(grp):
        for h in (2 * grp, 2 * grp + 1):
            for g in range(2):
                q = h % 2 * 2 + g
                mat[pl.ds(xlo * OWN + q, TOK, stride=HQ // 2), :] = atx[h, rows(2 * g + xlo)].astype(F32)
                attnx(h, g).wait_recv()
                mat[pl.ds(other * OWN + q, TOK, stride=HQ // 2), :] = atin[h, g].astype(F32)

    def f_terms(n):
        @pl.loop(n * 4 // PIECES_A, (n + 1) * 4 // PIECES_A)
        def _(m):
            rr = pl.ds(pl.multiple_of(m * 256, 256), 256)
            fst[rr, :] = nn(mat[rr, :].astype(BF16), cenw[...]).astype(BF16).astype(F32)

    def core_step(n, acc):
        def f_tok(t):
            r8 = pl.ds(pl.multiple_of(t * 8, 8), 8)
            return jnp.concatenate([fst[r8, b * HD : (b + 1) * HD] for b in range(BOND)], axis=0)

        cot4 = jnp.concatenate([cot_tok(4 * n + u) for u in range(4)], axis=1)
        return acc + nt(cot4, jnp.concatenate([f_tok(4 * n + u).astype(BF16) for u in range(4)], axis=1))

    def core_piece(item):
        kind, grp, n = item
        if kind == "A":
            if n == 0:
                attn_terms(grp)
            f_terms(n)
        else:
            steps = TOK // 4 // PIECES_G
            gacc[grp] = lax.fori_loop(n * steps, (n + 1) * steps, core_step, gacc[grp], unroll=2)

    def hook(h, name):
        for (n, point), todo in HOOKS.items():
            if point == name:

                @pl.when(h == n)
                def _():
                    for item in todo:
                        if item[0] == "f":
                            forward(*item[1:])
                        elif item[0] in "AG":
                            core_piece(item)
                        else:
                            back(*item[1:])

    @pl.loop(0, OWN)
    def _(h):
        for g in range(2):
            qx(h, g).wait_recv()
            qlocal(h, g).wait()
        hop(HOPS, h, 0).wait_recv()
        qh = qbuf[h]
        hook(h, "a")

        def scores(s, u):
            return nt(kv[s, h, 0, rows(u)], qh)

        m = jnp.full((1, COLS), MASK_FILL, F32)
        for u in range(2):
            causal = t_pos >= r_iota + u * TOK
            far = jnp.where(zpos >= HOPS, scores(HOPS, u), MASK_FILL)
            x = jnp.where(causal, scores(0, u), far)
            sc[u * TOK : (u + 1) * TOK, :] = x
            m = jnp.maximum(m, jnp.max(x, axis=0, keepdims=True))

        def score_step(w, m):
            s = w // 2
            x = jnp.where(zpos >= s, scores(s, lax.rem(w, 2)), MASK_FILL)
            sc[rows(w), :] = x
            return jnp.maximum(m, jnp.max(x, axis=0, keepdims=True))

        m = lax.fori_loop(2, 2 * HOPS, score_step, m)

        hook(h, "b")

        def exp_step(w, l):
            e = jnp.exp2((sc[rows(w), :] - m) * EXP_SCALE)
            sc[rows(w), :] = e
            return l + jnp.sum(e, axis=0, keepdims=True)

        l = lax.fori_loop(0, 2 * HOPS, exp_step, jnp.zeros((1, COLS), F32))
        inv = 1.0 / l
        hook(h, "c")
        hop(HOPS, h, 1).wait_recv()
        for s in range(HOPS + 1):
            for u in range(2):
                w = 2 * s + u
                vt[:, w * TOK : (w + 1) * TOK] = kv[s, h, 1, u * TOK : (u + 1) * TOK].T

        for u in range(2):
            causal = t_pos >= r_iota + u * TOK
            p = sc[u * TOK : (u + 1) * TOK, :] * inv
            sc[u * TOK : (u + 1) * TOK, :] = p
            ph[u * TOK : (u + 1) * TOK, :] = jnp.where(causal, p, 0.0).astype(BF16)
            w = 2 * HOPS + u
            ph[w * TOK : (w + 1) * TOK, :] = jnp.where(causal, 0.0, p).astype(BF16)

        @pl.loop(2, 2 * HOPS)
        def _(w):
            p = sc[rows(w), :] * inv
            sc[rows(w), :] = p
            ph[rows(w), :] = p.astype(BF16)

        hook(h, "d")
        for g in range(2):
            dax(h, g).wait_recv()
        dah = dabuf[h]
        dat[...] = dah.T
        att = nn(vt[...], ph[...]).astype(BF16)
        delta = jnp.sum(att.astype(F32) * dat[...].astype(F32), axis=0, keepdims=True)
        atx[h] = att.T
        for g in range(2):
            attnx(h, g).start()
        hook(h, "e")

        @pl.loop(0, HOPS + 1)
        def _(s):
            for u in range(2):
                part[h, s, 1, u * TOK : (u + 1) * TOK] = nn(ph[rows(2 * s + u), :], dah)

        hook(h, "f")

        def dprob(s, u):
            return nn(kv[s, h, 1, rows(u)], dat[...])

        for u in range(2):
            causal = t_pos >= r_iota + u * TOK
            dp = jnp.where(causal, dprob(0, u), dprob(HOPS, u))
            d = sc[u * TOK : (u + 1) * TOK, :] * (dp - delta)
            ds[u * TOK : (u + 1) * TOK, :] = jnp.where(causal, d, 0.0).astype(BF16)
            w = 2 * HOPS + u
            ds[w * TOK : (w + 1) * TOK, :] = jnp.where(causal, 0.0, d).astype(BF16)

        @pl.loop(2, 2 * HOPS)
        def _(w):
            dp = dprob(w // 2, lax.rem(w, 2))
            ds[rows(w), :] = (sc[rows(w), :] * (dp - delta)).astype(BF16)

        hook(h, "g")
        for s in range(HOPS + 1):
            for u in range(2):
                w = 2 * s + u
                kt[:, w * TOK : (w + 1) * TOK] = kv[s, h, 0, u * TOK : (u + 1) * TOK].T
        dqt = (nn(kt[...], ds[...]) * SCORE_SCALE).astype(BF16)
        dqx[h] = dqt.T
        for g in range(2):
            dqxc(h, g).start()
        for g in range(2):
            dq_ref[:, lanes(xlo * 2 * OWN + 2 * h + g)] = dqx[h, rows(2 * g + xlo)]

        @pl.loop(0, HOPS + 1)
        def _(s):
            for u in range(2):
                part[h, s, 0, u * TOK : (u + 1) * TOK] = nn(ds[rows(2 * s + u), :], qh) * SCORE_SCALE

        hook(h, "h")

    def reduce_copy(k, d, dev):
        pos = stage_peers(stages[k])[0]
        return remote(arbuf.at[k, pos], arbuf.at[k, pos], ar_s.at[k, d], ar_r.at[k, d], dev)

    def reduce_start(k):
        pos, peers = stage_peers(stages[k])
        arbuf[k, pos] = core_ref[...]
        for d, dev in peers:
            reduce_copy(k, d, dev).start()

    def reduce_end(k):
        for d, dev in stage_peers(stages[k])[1]:
            reduce_copy(k, d, dev).wait_recv()
        total = arbuf[k, 0]
        for n in range(1, stages[k][1] * stages[k][3]):
            total = total + arbuf[k, n]
        core_ref[...] = total
        for d, dev in stage_peers(stages[k])[1]:
            reduce_copy(k, d, dev).wait_send()

    reduced = -1
    for item in LAST:
        if item[0] in "AG":
            core_piece(item)
        elif item[0] == "b":
            back(*item[1:])
        elif item[1] < len(stages):
            if reduced >= 0:
                reduce_end(reduced)
            else:
                core_ref[...] = jnp.concatenate([gacc[0], gacc[1]], axis=1)
            reduced = item[1]
            reduce_start(reduced)
    reduce_end(reduced)

    for h in range(OWN):
        for c in range(2):
            kx(h, c).wait_send()
            qx(h, c).wait_send()
            dax(h, c).wait_send()
            attnx(h, c).wait_send()
            dqxc(h, c).wait()
            finc(h, c).wait()
            for s in range(HOPS):
                if s == 0 and h < SPLIT:
                    own(h, c).wait_send()
                    rest(h, c).wait_send()
                else:
                    hop(s + 1, h, c).wait_send()
                chain(s, h, c).wait_send()


def solution(mesh):
    n_ctx = mesh.shape["ctx"]
    stages = reduce_stages(mesh.shape)
    all_tokens = TOK * n_ctx * mesh.shape["dp"]

    def step(queries, key_states, value_states, cotangent, core_aux, core_central):
        aux = jnp.transpose(core_aux, (2, 0, 1)).reshape(BOND * HQ, J1)
        vm = pl.BlockSpec(memory_space=pltpu.VMEM)
        dma = pltpu.SemaphoreType.DMA
        pair = dma((OWN, 2))
        width = 2 * OWN * HD
        most = max(stage[1] * stage[3] for stage in stages)
        dq, dk, dv, core = pl.pallas_call(
            functools.partial(kernel, n_ctx, stages),
            out_shape=(
                jax.ShapeDtypeStruct((TOK, HQ * HD), BF16),
                jax.ShapeDtypeStruct((TOK, HK * HD), BF16),
                jax.ShapeDtypeStruct((TOK, HK * HD), BF16),
                jax.ShapeDtypeStruct((JP, BOND * HQ), F32),
            ),
            in_specs=[vm] * 6,
            out_specs=(vm, vm, vm, vm),
            scratch_shapes=[
                pltpu.VMEM((HOPS + 1, OWN, 2, BLK, HD), BF16),
                pltpu.VMEM((OWN, COLS, HD), BF16),
                pltpu.VMEM((OWN, COLS, HD), BF16),
                pltpu.VMEM((OWN, 2, TOK, HD), BF16),
                pltpu.VMEM((OWN, COLS, HD), BF16),
                pltpu.VMEM((OWN, 2, TOK, HD), BF16),
                pltpu.VMEM((OWN, COLS, HD), BF16),
                pltpu.VMEM((HOPS, OWN, 2, BLK, HD), BF16),
                pltpu.VMEM((HOPS, OWN, 2, BLK, HD), BF16),
                pltpu.VMEM((OWN, 2, TOK, HD), BF16),
                pltpu.VMEM((len(stages), most, JP, BOND * HQ), F32),
                pltpu.VMEM((BOND * HQ, JP), BF16),
                pltpu.VMEM((TOK * JP, HD), F32),
                pltpu.VMEM((TOK * HQ, BOND * HD), BF16),
                pltpu.VMEM((TOK * HQ // 2, BOND * HD), F32),
                pltpu.VMEM((2, JP, BOND * HQ // 2), F32),
                pltpu.VMEM((TOK * HQ, HD), F32),
                pltpu.VMEM((BOND * HD, HD), BF16),
                pltpu.VMEM((HD, BOND * HD), BF16),
                pltpu.VMEM((HD, (HOPS + 1) * BLK), BF16),
                pltpu.VMEM((HD, (HOPS + 1) * BLK), BF16),
                pltpu.VMEM((HD, COLS), BF16),
                pltpu.VMEM((HOPS * BLK, COLS), F32),
                pltpu.VMEM(((HOPS + 1) * BLK, COLS), BF16),
                pltpu.VMEM(((HOPS + 1) * BLK, COLS), BF16),
                pltpu.VMEM((OWN, HOPS + 1, 2, BLK, HD), F32),
                pair, pair, pair, pair, pair, pair,
                dma((HOPS, OWN, 2)), dma((HOPS, OWN, 2)),
                pair, pair, pair, pair, pair, pair,
                dma((HOPS, OWN, 2)), dma((HOPS, OWN, 2)),
                pair, pair,
                dma((len(stages), most)), dma((len(stages), most)),
                dma((SPLIT, 2)), dma((SPLIT, 2)),
            ],
            compiler_params=pltpu.CompilerParams(
                collective_id=0, has_side_effects=True, vmem_limit_bytes=60 * 1024 * 1024
            ),
        )(queries[0], key_states[0], value_states[0], cotangent[0], aux, core_central)
        core = jnp.transpose(core[:J1].reshape(J1, 2, BOND, 2, OWN), (3, 1, 4, 0, 2)).reshape(HQ, J1, BOND)
        core = core / jnp.sqrt(jnp.float32(all_tokens * HD))
        return dq[None], dk[None], dv[None], core

    return jax.shard_map(
        step,
        mesh=mesh,
        in_specs=(P("dp", "ctx", None),) * 4 + (P(), P()),
        out_specs=(P("dp", "ctx", None),) * 3 + (P(),),
        check_vma=False,
    )
```

```python
import functools
import math

import jax
import jax.numpy as jnp
from jax import lax
from jax.experimental import pallas as pl
from jax.experimental.pallas import tpu as pltpu
from jax.sharding import PartitionSpec as P

HD = 128
HQ = 16
HK = 8
J1 = 42
JP = 48
BOND = 8
WINDOW = 1024
TOK = 128
BLK = 2 * TOK
OWN = HK // 2
HOPS = WINDOW // BLK
COLS = 2 * BLK
SCORE_SCALE = 168.0 ** (-0.5)
EXP_SCALE = SCORE_SCALE * math.log2(math.e)
MASK_FILL = -1e30
F32 = jnp.float32
BF16 = jnp.bfloat16
MESH = pl.DeviceIdType.MESH
SPLIT = 2
PIECES_A = 2
PIECES_G = 4

FIRST = [
    "e", "e", "e", ("f", 1, 0, 0), "e", ("f", 1, 0, 1), "e", "e", ("f", 1, 1, 0), "e", ("f", 1, 1, 1), "e",
    ("f", 2, 0, 0), "e", ("f", 2, 0, 1), "e", ("f", 2, 1, 0), "e", "e", ("f", 3, 0, 0), "e", ("f", 3, 0, 1),
    "e", ("f", 2, 1, 1), "e", "e", ("f", 4, 0, 0), ("f", 3, 1, 0), "d", ("f", 4, 0, 1), ("f", 1, 2, 0),
    ("f", 3, 1, 1),
]
HOOKS = {
    (0, "c"): [("f", 1, 2, 1), ("f", 4, 1, 0)],
    (0, "f"): [("f", 2, 2, 0)],
    (0, "g"): [("b", 0, 0, 1), ("f", 4, 1, 1)],
    (0, "h"): [("f", 2, 2, 1), ("b", 0, 0, 0), ("f", 1, 3, 0)],
    (1, "b"): [("f", 3, 2, 0), ("b", 1, 0, 1), ("f", 1, 3, 1)],
    (1, "d"): [("b", 1, 0, 0)],
    (1, "f"): [("b", 0, 1, 1), ("f", 3, 2, 1)],
    (1, "g"): [("b", 2, 0, 1), ("f", 2, 3, 0), ("f", 4, 2, 0), ("A", 0, 0), ("b", 2, 0, 0)],
    (1, "h"): [("f", 2, 3, 1), ("b", 1, 1, 1), ("f", 4, 2, 1), ("A", 0, 1), ("b", 0, 1, 0), ("G", 0, 0), ("b", 3, 0, 1), ("f", 3, 3, 0)],
    (2, "b"): [("f", 3, 3, 1), ("b", 2, 1, 1)],
    (2, "d"): [("b", 1, 1, 0), ("b", 3, 0, 0), ("f", 4, 3, 0)],
    (2, "f"): [("b", 0, 2, 1)],
    (2, "g"): [("f", 4, 3, 1), ("b", 3, 1, 1)],
    (2, "h"): [("b", 0, 2, 0)],
    (3, "a"): [("b", 2, 1, 0)],
    (3, "c"): [("b", 1, 2, 1)],
    (3, "f"): [("b", 0, 3, 1)],
    (3, "g"): [("b", 1, 2, 0)],
}
LAST = [
    ("b", 0, 3, 0), ("G", 0, 1), ("b", 2, 2, 1), ("b", 3, 1, 0), ("G", 0, 2), ("G", 0, 3), ("A", 1, 0),
    ("b", 1, 3, 1), ("b", 1, 3, 0), ("A", 1, 1), ("G", 1, 0), ("b", 2, 2, 0), ("G", 1, 1), ("G", 1, 2),
    ("b", 3, 2, 1), ("G", 1, 3), ("a", 0), ("b", 2, 3, 1), ("b", 2, 3, 0), ("b", 3, 2, 0), ("a", 1),
    ("b", 4, 2, 1), ("b", 3, 3, 1), ("b", 3, 3, 0), ("a", 2), ("b", 4, 1, 1), ("b", 4, 3, 1), ("b", 4, 0, 1),
    ("b", 4, 1, 0), ("b", 4, 2, 0), ("b", 4, 0, 0), ("b", 4, 3, 0), ("a", 3),
]


def reduce_stages(mesh_shape):
    dp, ctx = mesh_shape["dp"], mesh_shape["ctx"]
    near = min(4, dp)
    stages = [(0, near, 0, 2), (2, dp // near, 0, 1)]
    rest, bit = ctx // 2, 1
    while rest > 1:
        size = min(4, rest)
        stages.append((0, 1, bit, size))
        rest, bit = rest // size, bit + 2
    return [stage for stage in stages if stage[1] * stage[3] > 1]


def nt(a, b):
    return lax.dot_general(a, b, (((1,), (1,)), ((), ())), preferred_element_type=F32)


def nn(a, b):
    return lax.dot_general(a, b, (((1,), (0,)), ((), ())), preferred_element_type=F32)


def lanes(start):
    return pl.ds(pl.multiple_of(start * HD, HD), HD)


def rows(start):
    return pl.ds(pl.multiple_of(start * TOK, TOK), TOK)


def kernel(
    n_ctx, stages,
    q_ref, k_ref, v_ref, cot_ref, aux_ref, cen_ref,
    dq_ref, dk_ref, dv_ref, core_ref,
    kv, qbuf, dabuf, dasend, atx, atin, dqx, csend, crecv, finx, arbuf,
    aux, cots, est, fst, gacc, mat, cent, cenw, kt, vt, dat, sc, ph, ds, part,
    kx_s, kx_r, loc, qx_s, qx_r, qloc, hop_s, hop_r, da_s, da_r, at_s, at_r,
    dq_s, dq_r, ch_s, ch_r, fin_s, fin_r, ar_s, ar_r, own_s, own_r,
):
    me_dp = lax.axis_index("dp")
    me = lax.axis_index("ctx")
    zpos = me // 2
    xlo = lax.rem(me, 2)
    other = 1 - xlo
    partner = {"ctx": me + 1 - 2 * xlo}
    up = {"ctx": lax.rem(me + 2, n_ctx)}
    down = {"ctx": lax.rem(me + n_ctx - 2, n_ctx)}

    def stage_peers(stage):
        dp_bit, dp_size, ctx_bit, ctx_size = stage
        size = dp_size * ctx_size
        dp_pos = lax.rem(me_dp // (1 << dp_bit), dp_size)
        ctx_pos = lax.rem(me // (1 << ctx_bit), ctx_size)
        pos = dp_pos * ctx_size + ctx_pos
        out = []
        for d in range(1, size):
            their = lax.rem(pos + d, size)
            dev = {
                "dp": me_dp + (their // ctx_size - dp_pos) * (1 << dp_bit),
                "ctx": me + (lax.rem(their, ctx_size) - ctx_pos) * (1 << ctx_bit),
            }
            out.append((d, dev))
        return pos, out

    def remote(src, dst, s, r, dev):
        return pltpu.make_async_remote_copy(
            src_ref=src, dst_ref=dst, send_sem=s, recv_sem=r, device_id=dev, device_id_type=MESH
        )

    barrier = pltpu.get_barrier_semaphore()
    greet = [partner, up, down]
    for stage in (stage for stage in stages if stage[2] == 0):
        greet += [dev for _, dev in stage_peers(stage)[1]]
    for dev in greet:
        pl.semaphore_signal(barrier, inc=1, device_id=dev, device_id_type=MESH)
    pl.semaphore_wait(barrier, len(greet))

    srcs = (k_ref, v_ref)

    def kx(h, c):
        return remote(
            srcs[c].at[:, lanes(other * OWN + h)], kv.at[0, h, c, rows(xlo)],
            kx_s.at[h, c], kx_r.at[h, c], partner,
        )

    def kloc(h, c):
        return pltpu.make_async_copy(
            srcs[c].at[:, lanes(xlo * OWN + h)], kv.at[0, h, c, rows(xlo)], loc.at[h, c]
        )

    def qx(h, g):
        return remote(
            q_ref.at[:, lanes(other * 2 * OWN + 2 * h + g)], qbuf.at[h, rows(2 * g + xlo)],
            qx_s.at[h, g], qx_r.at[h, g], partner,
        )

    def qlocal(h, g):
        return pltpu.make_async_copy(
            q_ref.at[:, lanes(xlo * 2 * OWN + 2 * h + g)], qbuf.at[h, rows(2 * g + xlo)], qloc.at[h, g]
        )

    def own(h, c):
        return remote(
            srcs[c].at[:, lanes(xlo * OWN + h)], kv.at[1, h, c, rows(xlo)],
            own_s.at[h, c], own_r.at[h, c], up,
        )

    def rest(h, c):
        return remote(
            kv.at[0, h, c, rows(other)], kv.at[1, h, c, rows(other)],
            hop_s.at[0, h, c], hop_r.at[0, h, c], up,
        )

    def hop(s, h, c):
        return remote(kv.at[s - 1, h, c], kv.at[s, h, c], hop_s.at[s - 1, h, c], hop_r.at[s - 1, h, c], up)

    def dax(h, g):
        return remote(
            dasend.at[h, g], dabuf.at[h, rows(2 * g + xlo)], da_s.at[h, g], da_r.at[h, g], partner
        )

    def attnx(h, g):
        return remote(
            atx.at[h, rows(2 * g + other)], atin.at[h, g], at_s.at[h, g], at_r.at[h, g], partner
        )

    def dqxc(h, g):
        return remote(
            dqx.at[h, rows(2 * g + other)], dq_ref.at[:, lanes(xlo * 2 * OWN + 2 * h + g)],
            dq_s.at[h, g], dq_r.at[h, g], partner,
        )

    def chain(st, h, c):
        return remote(
            csend.at[st, h, c], crecv.at[st, h, c], ch_s.at[st, h, c], ch_r.at[st, h, c], down
        )

    outs = (dk_ref, dv_ref)

    def finc(h, c):
        return remote(
            finx.at[h, c], outs[c].at[:, lanes(xlo * OWN + h)], fin_s.at[h, c], fin_r.at[h, c], partner
        )

    for h in range(OWN):
        for c in range(2):
            kx(h, c).start()
            kloc(h, c).start()
            if h < SPLIT:
                own(h, c).start()
    for h in range(OWN):
        for c in range(2):
            qx(h, c).start()
            qlocal(h, c).start()

    aux[...] = jnp.zeros(aux.shape, BF16)
    aux[:, :J1] = aux_ref[...]
    gacc[...] = jnp.zeros(gacc.shape, F32)

    @pl.loop(0, TOK)
    def _(t):
        cots[pl.ds(t * JP + JP - 8, 8), :] = jnp.zeros((8, HD), F32)

    @pl.loop(0, J1)
    def _(j):
        cots[pl.ds(j, TOK, stride=JP), :] = cot_ref[:, lanes(j)].astype(F32)

    @pl.loop(0, BOND)
    def _(b):
        cent[rows(b), :] = cen_ref[b].T
        cenw[:, lanes(b)] = cen_ref[b]

    def cot_tok(t):
        return cots[pl.ds(pl.multiple_of(t * JP, JP), JP), :].astype(BF16)

    def e_terms(t):
        e = nn(aux[...], jnp.concatenate([cot_tok(t), cot_tok(t + 1)], axis=1)).astype(BF16)
        for u in range(2):
            r16 = pl.ds(pl.multiple_of((t + u) * HQ, HQ), HQ)
            for b in range(BOND):
                est[r16, b * HD : (b + 1) * HD] = e[b * HQ : (b + 1) * HQ, u * HD : (u + 1) * HD]

    def forward(s, h, c):
        if s == 1:
            kx(h, c).wait_recv()
            kloc(h, c).wait()
        elif s == 2 and h < SPLIT:
            own(h, c).wait_recv()
            rest(h, c).wait_recv()
        else:
            hop(s - 1, h, c).wait_recv()
        if s == 1 and h < SPLIT:
            rest(h, c).start()
        else:
            hop(s, h, c).start()

    def d_terms():
        @pl.loop(0, 8)
        def _(n):
            rr = pl.ds(pl.multiple_of(n * 256, 256), 256)
            mat[rr, :] = nn(est[rr, :], cent[...]).astype(BF16).astype(F32)

        for h in range(OWN):
            for g in range(2):
                i_other = other * 2 * OWN + 2 * h + g
                dasend[h, g] = mat[pl.ds(i_other, TOK, stride=HQ), :].astype(BF16)
        for h in range(OWN):
            for g in range(2):
                dax(h, g).start()
        for h in range(OWN):
            for g in range(2):
                i_own = xlo * 2 * OWN + 2 * h + g
                dabuf[h, rows(2 * g + xlo)] = mat[pl.ds(i_own, TOK, stride=HQ), :].astype(BF16)

    pieces = TOK // FIRST.count("e")
    done = 0
    for item in FIRST:
        if item == "e":

            @pl.loop(done // 2, (done + pieces) // 2, unroll=4)
            def _(n):
                e_terms(2 * n)

            done += pieces
        elif item == "d":
            d_terms()
        else:
            forward(*item[1:])

    t_pos = lax.rem(lax.broadcasted_iota(jnp.int32, (TOK, COLS), 1), BLK)
    r_iota = lax.broadcasted_iota(jnp.int32, (TOK, COLS), 0)

    def back(st, hh, c):
        total = part[hh, HOPS - st, c]
        if st > 0:
            chain(st - 1, hh, c).wait_recv()
            total = crecv[st - 1, hh, c].astype(F32) + total
        total = total.astype(BF16)
        if st < HOPS:
            csend[st, hh, c] = total
            chain(st, hh, c).start()
        else:
            part[hh, 0, c] = total.astype(F32)
            finx[hh, c] = part[hh, 0, c, rows(other)].astype(BF16)
            finc(hh, c).start()
            outs[c][:, lanes(xlo * OWN + hh)] = part[hh, 0, c, rows(xlo)].astype(BF16)

    def attn_terms(grp):
        for h in (2 * grp, 2 * grp + 1):
            for g in range(2):
                q = h % 2 * 2 + g
                mat[pl.ds(xlo * OWN + q, TOK, stride=HQ // 2), :] = atx[h, rows(2 * g + xlo)].astype(F32)
                attnx(h, g).wait_recv()
                mat[pl.ds(other * OWN + q, TOK, stride=HQ // 2), :] = atin[h, g].astype(F32)

    def f_terms(n):
        @pl.loop(n * 4 // PIECES_A, (n + 1) * 4 // PIECES_A)
        def _(m):
            rr = pl.ds(pl.multiple_of(m * 256, 256), 256)
            fst[rr, :] = nn(mat[rr, :].astype(BF16), cenw[...]).astype(BF16).astype(F32)

    def core_step(n, acc):
        def f_tok(t):
            r8 = pl.ds(pl.multiple_of(t * 8, 8), 8)
            return jnp.concatenate([fst[r8, b * HD : (b + 1) * HD] for b in range(BOND)], axis=0)

        cot4 = jnp.concatenate([cot_tok(4 * n + u) for u in range(4)], axis=1)
        return acc + nt(cot4, jnp.concatenate([f_tok(4 * n + u).astype(BF16) for u in range(4)], axis=1))

    def core_piece(item):
        kind, grp, n = item
        if kind == "A":
            if n == 0:
                attn_terms(grp)
            f_terms(n)
        else:
            steps = TOK // 4 // PIECES_G
            gacc[grp] = lax.fori_loop(n * steps, (n + 1) * steps, core_step, gacc[grp], unroll=2)

    def hook(h, name):
        for (n, point), todo in HOOKS.items():
            if point == name:

                @pl.when(h == n)
                def _():
                    for item in todo:
                        if item[0] == "f":
                            forward(*item[1:])
                        elif item[0] in "AG":
                            core_piece(item)
                        else:
                            back(*item[1:])

    @pl.loop(0, OWN)
    def _(h):
        for g in range(2):
            qx(h, g).wait_recv()
            qlocal(h, g).wait()
        hop(HOPS, h, 0).wait_recv()
        qh = qbuf[h]
        hook(h, "a")

        def scores(s, u):
            return nt(kv[s, h, 0, rows(u)], qh)

        m = jnp.full((1, COLS), MASK_FILL, F32)
        for u in range(2):
            causal = t_pos >= r_iota + u * TOK
            far = jnp.where(zpos >= HOPS, scores(HOPS, u), MASK_FILL)
            x = jnp.where(causal, scores(0, u), far)
            sc[u * TOK : (u + 1) * TOK, :] = x
            m = jnp.maximum(m, jnp.max(x, axis=0, keepdims=True))

        def score_step(w, m):
            s = w // 2
            x = jnp.where(zpos >= s, scores(s, lax.rem(w, 2)), MASK_FILL)
            sc[rows(w), :] = x
            return jnp.maximum(m, jnp.max(x, axis=0, keepdims=True))

        m = lax.fori_loop(2, 2 * HOPS, score_step, m)

        hook(h, "b")

        def exp_step(w, l):
            e = jnp.exp2((sc[rows(w), :] - m) * EXP_SCALE)
            sc[rows(w), :] = e
            return l + jnp.sum(e, axis=0, keepdims=True)

        l = lax.fori_loop(0, 2 * HOPS, exp_step, jnp.zeros((1, COLS), F32))
        inv = 1.0 / l
        hook(h, "c")
        hop(HOPS, h, 1).wait_recv()
        for s in range(HOPS + 1):
            for u in range(2):
                w = 2 * s + u
                vt[:, w * TOK : (w + 1) * TOK] = kv[s, h, 1, u * TOK : (u + 1) * TOK].T

        for u in range(2):
            causal = t_pos >= r_iota + u * TOK
            p = sc[u * TOK : (u + 1) * TOK, :] * inv
            sc[u * TOK : (u + 1) * TOK, :] = p
            ph[u * TOK : (u + 1) * TOK, :] = jnp.where(causal, p, 0.0).astype(BF16)
            w = 2 * HOPS + u
            ph[w * TOK : (w + 1) * TOK, :] = jnp.where(causal, 0.0, p).astype(BF16)

        @pl.loop(2, 2 * HOPS)
        def _(w):
            p = sc[rows(w), :] * inv
            sc[rows(w), :] = p
            ph[rows(w), :] = p.astype(BF16)

        hook(h, "d")
        for g in range(2):
            dax(h, g).wait_recv()
        dah = dabuf[h]
        dat[...] = dah.T
        att = nn(vt[...], ph[...]).astype(BF16)
        delta = jnp.sum(att.astype(F32) * dat[...].astype(F32), axis=0, keepdims=True)
        atx[h] = att.T
        for g in range(2):
            attnx(h, g).start()
        hook(h, "e")

        @pl.loop(0, HOPS + 1)
        def _(s):
            for u in range(2):
                part[h, s, 1, u * TOK : (u + 1) * TOK] = nn(ph[rows(2 * s + u), :], dah)

        hook(h, "f")

        def dprob(s, u):
            return nn(kv[s, h, 1, rows(u)], dat[...])

        for u in range(2):
            causal = t_pos >= r_iota + u * TOK
            dp = jnp.where(causal, dprob(0, u), dprob(HOPS, u))
            d = sc[u * TOK : (u + 1) * TOK, :] * (dp - delta)
            ds[u * TOK : (u + 1) * TOK, :] = jnp.where(causal, d, 0.0).astype(BF16)
            w = 2 * HOPS + u
            ds[w * TOK : (w + 1) * TOK, :] = jnp.where(causal, 0.0, d).astype(BF16)

        @pl.loop(2, 2 * HOPS)
        def _(w):
            dp = dprob(w // 2, lax.rem(w, 2))
            ds[rows(w), :] = (sc[rows(w), :] * (dp - delta)).astype(BF16)

        hook(h, "g")
        for s in range(HOPS + 1):
            for u in range(2):
                w = 2 * s + u
                kt[:, w * TOK : (w + 1) * TOK] = kv[s, h, 0, u * TOK : (u + 1) * TOK].T
        dqt = (nn(kt[...], ds[...]) * SCORE_SCALE).astype(BF16)
        dqx[h] = dqt.T
        for g in range(2):
            dqxc(h, g).start()
        for g in range(2):
            dq_ref[:, lanes(xlo * 2 * OWN + 2 * h + g)] = dqx[h, rows(2 * g + xlo)]

        @pl.loop(0, HOPS + 1)
        def _(s):
            for u in range(2):
                part[h, s, 0, u * TOK : (u + 1) * TOK] = nn(ds[rows(2 * s + u), :], qh) * SCORE_SCALE

        hook(h, "h")

    def reduce_copy(k, d, dev):
        pos = stage_peers(stages[k])[0]
        return remote(arbuf.at[k, pos], arbuf.at[k, pos], ar_s.at[k, d], ar_r.at[k, d], dev)

    def reduce_start(k):
        pos, peers = stage_peers(stages[k])
        arbuf[k, pos] = core_ref[...]
        for d, dev in peers:
            reduce_copy(k, d, dev).start()

    def reduce_end(k):
        for d, dev in stage_peers(stages[k])[1]:
            reduce_copy(k, d, dev).wait_recv()
        total = arbuf[k, 0]
        for n in range(1, stages[k][1] * stages[k][3]):
            total = total + arbuf[k, n]
        core_ref[...] = total
        for d, dev in stage_peers(stages[k])[1]:
            reduce_copy(k, d, dev).wait_send()

    reduced = -1
    for item in LAST:
        if item[0] in "AG":
            core_piece(item)
        elif item[0] == "b":
            back(*item[1:])
        elif item[1] < len(stages):
            if reduced >= 0:
                reduce_end(reduced)
            else:
                core_ref[...] = jnp.concatenate([gacc[0], gacc[1]], axis=1)
            reduced = item[1]
            reduce_start(reduced)
    reduce_end(reduced)

    for h in range(OWN):
        for c in range(2):
            kx(h, c).wait_send()
            qx(h, c).wait_send()
            dax(h, c).wait_send()
            attnx(h, c).wait_send()
            dqxc(h, c).wait()
            finc(h, c).wait()
            for s in range(HOPS):
                if s == 0 and h < SPLIT:
                    own(h, c).wait_send()
                    rest(h, c).wait_send()
                else:
                    hop(s + 1, h, c).wait_send()
                chain(s, h, c).wait_send()


def solution(mesh):
    n_ctx = mesh.shape["ctx"]
    stages = reduce_stages(mesh.shape)
    all_tokens = TOK * n_ctx * mesh.shape["dp"]

    def step(queries, key_states, value_states, cotangent, core_aux, core_central):
        aux = jnp.transpose(core_aux, (2, 0, 1)).reshape(BOND * HQ, J1)
        vm = pl.BlockSpec(memory_space=pltpu.VMEM)
        dma = pltpu.SemaphoreType.DMA
        pair = dma((OWN, 2))
        width = 2 * OWN * HD
        most = max(stage[1] * stage[3] for stage in stages)
        dq, dk, dv, core = pl.pallas_call(
            functools.partial(kernel, n_ctx, stages),
            out_shape=(
                jax.ShapeDtypeStruct((TOK, HQ * HD), BF16),
                jax.ShapeDtypeStruct((TOK, HK * HD), BF16),
                jax.ShapeDtypeStruct((TOK, HK * HD), BF16),
                jax.ShapeDtypeStruct((JP, BOND * HQ), F32),
            ),
            in_specs=[vm] * 6,
            out_specs=(vm, vm, vm, vm),
            scratch_shapes=[
                pltpu.VMEM((HOPS + 1, OWN, 2, BLK, HD), BF16),
                pltpu.VMEM((OWN, COLS, HD), BF16),
                pltpu.VMEM((OWN, COLS, HD), BF16),
                pltpu.VMEM((OWN, 2, TOK, HD), BF16),
                pltpu.VMEM((OWN, COLS, HD), BF16),
                pltpu.VMEM((OWN, 2, TOK, HD), BF16),
                pltpu.VMEM((OWN, COLS, HD), BF16),
                pltpu.VMEM((HOPS, OWN, 2, BLK, HD), BF16),
                pltpu.VMEM((HOPS, OWN, 2, BLK, HD), BF16),
                pltpu.VMEM((OWN, 2, TOK, HD), BF16),
                pltpu.VMEM((len(stages), most, JP, BOND * HQ), F32),
                pltpu.VMEM((BOND * HQ, JP), BF16),
                pltpu.VMEM((TOK * JP, HD), F32),
                pltpu.VMEM((TOK * HQ, BOND * HD), BF16),
                pltpu.VMEM((TOK * HQ // 2, BOND * HD), F32),
                pltpu.VMEM((2, JP, BOND * HQ // 2), F32),
                pltpu.VMEM((TOK * HQ, HD), F32),
                pltpu.VMEM((BOND * HD, HD), BF16),
                pltpu.VMEM((HD, BOND * HD), BF16),
                pltpu.VMEM((HD, (HOPS + 1) * BLK), BF16),
                pltpu.VMEM((HD, (HOPS + 1) * BLK), BF16),
                pltpu.VMEM((HD, COLS), BF16),
                pltpu.VMEM((HOPS * BLK, COLS), F32),
                pltpu.VMEM(((HOPS + 1) * BLK, COLS), BF16),
                pltpu.VMEM(((HOPS + 1) * BLK, COLS), BF16),
                pltpu.VMEM((OWN, HOPS + 1, 2, BLK, HD), F32),
                pair, pair, pair, pair, pair, pair,
                dma((HOPS, OWN, 2)), dma((HOPS, OWN, 2)),
                pair, pair, pair, pair, pair, pair,
                dma((HOPS, OWN, 2)), dma((HOPS, OWN, 2)),
                pair, pair,
                dma((len(stages), most)), dma((len(stages), most)),
                dma((SPLIT, 2)), dma((SPLIT, 2)),
            ],
            compiler_params=pltpu.CompilerParams(
                collective_id=0, has_side_effects=True, vmem_limit_bytes=60 * 1024 * 1024
            ),
        )(queries[0], key_states[0], value_states[0], cotangent[0], aux, core_central)
        core = jnp.transpose(core[:J1].reshape(J1, 2, BOND, 2, OWN), (3, 1, 4, 0, 2)).reshape(HQ, J1, BOND)
        core = core / jnp.sqrt(jnp.float32(all_tokens * HD))
        return dq[None], dk[None], dv[None], core

    return jax.shard_map(
        step,
        mesh=mesh,
        in_specs=(P("dp", "ctx", None),) * 4 + (P(), P()),
        out_specs=(P("dp", "ctx", None),) * 3 + (P(),),
        check_vma=False,
    )
```
